256 devices in a mesh: ep: 16 (over x, z_lo), etp: 2 (over z_hi), dp: 8 (over y, core).
Axes of the slice: x: 4, y: 4, z: 8 (z_hi: 2, z_lo: 4; z = z_hi * 4 + z_lo), core: 2. Of those that a mesh axis runs over, the one named last changes fastest.
Arguments:
- tokens: bfloat16 [8192, 4096], P(('ep', 'dp'), 'etp'), may hold values from -6 to 6
- expert_ids: int32 [8192, 8], P(('ep', 'dp')), may hold values from 0 to 15, all different within a row
- gate_weights: float32 [8192, 8], P(('ep', 'dp')), may hold values from 0.05 to 1
- up_weights: bfloat16 [16, 4096, 2, 1024], P('ep', None, None, 'etp'), may hold values from -0.09375 to 0.09375
- down_weights: bfloat16 [16, 1024, 4096], P('ep', 'etp'), may hold values from -0.1875 to 0.1875
Outputs:
- mixed: bfloat16 [8192, 4096], P(('ep', 'dp'), 'etp')
The draws below stay inside these ranges and needn't reach their ends.
Inputs may be any that keep to these rules, and one draw needn't show every extreme that they name: `expert_ids`: each token names 8 different experts.
All inputs are finite; a program needn't handle non-finite values.
Results may differ from the reference program's by a relative error of at most 0.0065.
Values may be sent and summed in bfloat16 or wider, within the bound.
No kernel may reach another device: no remote copies, remote signals or barrier semaphores. Data moves between devices by JAX's collectives and lax.ppermute only.
A program may use at most 128 MiB of HBM per device.

```python
import math
import jax
import jax.numpy as jnp
from jax import lax

D = 4096
FF = 1024
TOP = 8
EXPERTS = 16
TOKENS = 8192
N_ETP = 2


def levels(rng, shape, shards, smallest, largest):
    factor_of, own = 1.0, jax.random.fold_in(rng, 6)
    for dim, parts in shards:
        steps = jnp.exp(jax.random.uniform(jax.random.fold_in(own, dim), (parts,), jnp.float32, smallest / len(shards), largest / len(shards)))
        factor_of = factor_of * jnp.repeat(steps, shape[dim] // parts).reshape([-1 if axis == dim else 1 for axis in range(len(shape))])
    return factor_of


def different_ones(stream_key, rows, count, top, lift):
    order = jax.random.permutation(jax.random.fold_in(stream_key, 1), count)
    favour = order
    for power in range(3):
        favour = favour * favour // count
    favour = favour * lift // count
    chance = jax.random.randint(jax.random.fold_in(stream_key, 2), (rows, count), 0, 4096) + favour
    sure = jax.random.permutation(jax.random.fold_in(stream_key, 3), rows)[jnp.arange(count) % rows]
    chance = jnp.where(jnp.arange(rows)[:, None] == sure[None, :], 1 << 14, chance)
    score = chance * count + jnp.arange(count)
    return lax.top_k(score.astype(jnp.int32), top)[1].astype(jnp.int32)


def bell_draw(key, dims, deviation, bound, cuts=(), kind=jnp.bfloat16):
    drawn = deviation * jax.random.normal(key, dims, jnp.float32)
    if cuts:
        drawn = drawn * levels(key, dims, cuts, -0.22, 0.18)
    return jnp.clip(drawn, -bound, bound).astype(kind)


def setup_inputs(seed: int = 0) -> dict:
    streams_of = jax.random.split(jax.random.key(seed), 6)
    return {
        "tokens": bell_draw(streams_of[0], (TOKENS, D), 1.0, 6.0, ((0, 128), (1, 2))),
        "expert_ids": different_ones(streams_of[1], TOKENS, EXPERTS, TOP, 8192),
        "gate_weights": jnp.clip(jnp.exp(math.log(1.0) - 2.9957323 * jax.random.uniform(streams_of[2], (TOKENS, TOP), jnp.float32) ** levels(streams_of[2], (TOKENS, TOP), ((0, 128),), -0.2, 0.2)), 0.05, 1.0),
        "up_weights": bell_draw(streams_of[3], (EXPERTS, D, 2, FF), D ** -0.5, 0.09375, ((0, 16), (3, 2))),
        "down_weights": bell_draw(streams_of[4], (EXPERTS, FF, D), FF ** -0.5, 0.1875, ((0, 16), (1, 2))),
    }


def reference(tokens, expert_ids, gate_weights, up_weights, down_weights):
    buffer_rows = TOKENS
    pair_width = FF // N_ETP
    token_row = jnp.arange(TOKENS).astype(jnp.int32)

    def expert_step(running, expert_in):
        expert_up, expert_down, expert_num = expert_in
        picked = expert_ids == expert_num
        chosen = jnp.any(picked, axis=1)
        weight = jnp.sum(jnp.where(picked, gate_weights, jnp.float32(0.0)), axis=1)
        position = jnp.where(chosen, token_row, buffer_rows).astype(jnp.int32)
        buffer = jnp.zeros((buffer_rows, D), jnp.bfloat16).at[position].set(tokens, mode="drop")
        gate_act = jnp.dot(buffer, expert_up[:, 0, :], preferred_element_type=jnp.float32)
        up_act = jnp.dot(buffer, expert_up[:, 1, :], preferred_element_type=jnp.float32)
        hidden = (jax.nn.silu(gate_act) * up_act).astype(jnp.bfloat16)
        summed = jnp.zeros((buffer_rows, D), jnp.float32)
        for piece in range(N_ETP):
            partial_value = jnp.dot(hidden[:, piece * pair_width:(piece + 1) * pair_width],
                              expert_down[piece * pair_width:(piece + 1) * pair_width, :],
                              preferred_element_type=jnp.float32).astype(jnp.bfloat16)
            partial_value = lax.optimization_barrier(partial_value)
            summed = summed + partial_value.astype(jnp.float32)
        expert_rows = summed.astype(jnp.bfloat16)
        fetched = expert_rows[jnp.minimum(position, buffer_rows - 1)].astype(jnp.float32)
        return running + weight[:, None] * fetched, None

    running, _ = lax.scan(expert_step, jnp.zeros((TOKENS, D), jnp.float32),
                          (up_weights, down_weights, jnp.arange(EXPERTS).astype(jnp.int32)))
    return running.astype(jnp.bfloat16)
```

```python
import functools

import jax
import jax.numpy as jnp
from jax import lax
from jax.experimental import pallas as pl
from jax.experimental.pallas import tpu as pltpu
from jax.sharding import Mesh
from jax.sharding import PartitionSpec as P

ZAX = ("zl", "zh")
BF = jnp.bfloat16
F32 = jnp.float32


def permute_x(v, step):
    return lax.ppermute(v, "x", [(i, (i + step) % 4) for i in range(4)])


def permute_z(v, step):
    index = lambda z: (z % 4) * 2 + z // 4
    return lax.ppermute(v, ZAX, [(index(z), index((z + step) % 8)) for z in range(8)])


def halves(v):
    n = v.shape[0] // 2
    return v[:n], v[n:]


def gather_x(v):
    from_left = permute_x(v, 1)
    from_right = permute_x(v, -1)
    far0 = permute_x(halves(from_left)[0], 1)
    far1 = permute_x(halves(from_right)[1], -1)
    return v, from_right, (far0, far1), from_left


def gather_z(v):
    left, right = [v], [v]
    for _ in range(3):
        left.append(permute_z(left[-1], 1))
        right.append(permute_z(right[-1], -1))
    far0 = permute_z(halves(left[3])[0], 1)
    far1 = permute_z(halves(right[3])[1], -1)
    return [v, right[1], right[2], right[3], (far0, far1), left[3], left[2], left[1]]


def add(a, b):
    return (a.astype(F32) + b.astype(F32)).astype(BF)


def add_half(part, whole, which):
    w0, w1 = halves(whole)
    if which == 0:
        return jnp.concatenate([add(part, w0), w1])
    return jnp.concatenate([w0, add(part, w1)])


def scatter_x(y, own):
    to_right = permute_x(halves(y[2])[0], 1)
    to_left = permute_x(halves(y[2])[1], -1)
    to_right = permute_x(add_half(to_right, y[1], 0), 1)
    to_left = permute_x(add_half(to_left, y[3], 1), -1)
    return own.astype(F32) + to_right.astype(F32) + to_left.astype(F32)


def scatter_z(y, own):
    to_right = permute_z(halves(y[4])[0], 1)
    to_left = permute_z(halves(y[4])[1], -1)
    to_right = permute_z(add_half(to_right, y[3], 0), 1)
    to_left = permute_z(add_half(to_left, y[5], 1), -1)
    to_right = permute_z(add(to_right, y[2]), 1)
    to_left = permute_z(add(to_left, y[6]), -1)
    to_right = permute_z(add(to_right, y[1]), 1)
    to_left = permute_z(add(to_left, y[7]), -1)
    return own.astype(F32) + to_right.astype(F32) + to_left.astype(F32)


def expert_kernel(plan, n_in, n_out, z_ref, w_ref, *refs):
    ins = refs[:n_in]
    up_ref, down_ref = refs[n_in : n_in + 2]
    outs = refs[n_in + 2 : n_in + 2 + n_out]
    x_buf, up_buf, down_buf, hidden, y_buf, sem_x, sem_w, sem_y = refs[n_in + 2 + n_out :]
    z = z_ref[0]
    in_plan, out_plan = plan

    def where(d, row_of):
        at = lax.rem(z + d, 8)
        zl, zh = lax.rem(at, 4), lax.div(at, 4)
        return row_of(zl), pl.multiple_of(zh * 2048, 2048)

    copies = []
    for ref, start, rows, d, row_of in in_plan:
        row, col = where(d, row_of)
        copies.append(
            pltpu.make_async_copy(
                ins[ref].at[pl.ds(start, rows)],
                x_buf.at[pl.ds(row, rows), pl.ds(col, 2048)],
                sem_x,
            )
        )
    up_copy = pltpu.make_async_copy(up_ref, up_buf, sem_w.at[0])
    down_copy = pltpu.make_async_copy(down_ref, down_buf, sem_w.at[1])
    up_copy.start()
    for c in copies:
        c.start()
    down_copy.start()
    for c in copies:
        c.wait()
    up_copy.wait()

    def up_step(n, _):
        at = pl.ds(pl.multiple_of(n * 256, 256), 256)
        gate = jnp.dot(x_buf[...], up_buf[0, :, at], preferred_element_type=F32)
        up = jnp.dot(x_buf[...], up_buf[1, :, at], preferred_element_type=F32)
        hidden[:, at] = (gate / (1.0 + jnp.exp(-gate)) * up).astype(BF)
        return 0

    lax.fori_loop(0, 2, up_step, 0)
    down_copy.wait()
    w = w_ref[...]

    def down_step(n, _):
        at = pl.ds(pl.multiple_of(n * 256, 256), 256)
        y = jnp.dot(hidden[...], down_buf[:, at], preferred_element_type=F32)
        y_buf[:, at] = (y * w).astype(BF)
        return 0

    lax.fori_loop(0, 16, down_step, 0)
    copies = []
    for ref, start, rows, d, row_of in out_plan:
        row, col = where(d, row_of)
        copies.append(
            pltpu.make_async_copy(
                y_buf.at[pl.ds(row, rows), pl.ds(col, 2048)],
                outs[ref].at[pl.ds(start, rows)],
                sem_y,
            )
        )
    for c in copies:
        c.start()
    for c in copies:
        c.wait()


def expert(z, weight, pieces, up, down, plan, out_rows, name):
    n_in, n_out = len(pieces), len(out_rows)
    any_spec = pl.BlockSpec(memory_space=pl.ANY)
    return pl.pallas_call(
        functools.partial(expert_kernel, plan, n_in, n_out),
        out_shape=[jax.ShapeDtypeStruct((r, 2048), BF) for r in out_rows],
        in_specs=[
            pl.BlockSpec(memory_space=pltpu.SMEM),
            pl.BlockSpec(memory_space=pltpu.VMEM),
        ]
        + [any_spec] * (n_in + 2),
        out_specs=[any_spec] * n_out,
        scratch_shapes=[
            pltpu.VMEM((512, 4096), BF),
            pltpu.VMEM((2, 4096, 512), BF),
            pltpu.VMEM((512, 4096), BF),
            pltpu.VMEM((512, 512), BF),
            pltpu.VMEM((512, 4096), BF),
            pltpu.SemaphoreType.DMA,
            pltpu.SemaphoreType.DMA((2,)),
            pltpu.SemaphoreType.DMA,
        ],
        compiler_params=pltpu.CompilerParams(vmem_limit_bytes=48 << 20),
        name=name,
    )(z, weight, *pieces, up, down)


def mult(v, k):
    return pl.multiple_of(v * k, k)


def plan_a():
    ins, outs = [], []
    ref = 0
    for d in range(8):
        if d == 4:
            ins.append((ref, 0, 64, d, lambda zl: mult(zl, 128)))
            ins.append((ref + 1, 0, 64, d, lambda zl: mult(zl, 128) + 64))
            ref += 2
        else:
            ins.append((ref, 0, 128, d, lambda zl: mult(zl, 128)))
            ref += 1
        outs.append((d, 0, 128, d, lambda zl: mult(zl, 128)))
    return ins, outs


def plan_b():
    ins, outs = [], []
    for xr in range(4):
        for d in range(8):
            ref, start = {0: 0, 1: 1, 2: 2, 3: 4}[xr], d * 32
            if xr == 2 and d >= 4:
                ref, start = 3, (d - 4) * 32
            row_of = lambda zl, xr=xr: xr * 128 + mult(zl, 32)
            ins.append((ref, start, 32, d, row_of))
            outs.append((xr, d * 32, 32, d, row_of))
    return ins, outs


def local(tokens, expert_ids, gate_weights, up_weights, down_weights):
    x, zl, zh = lax.axis_index("x"), lax.axis_index("zl"), lax.axis_index("zh")
    z = zh * 4 + zl
    expert_num = x * 4 + zl
    picked = expert_ids[:, :, None] == jnp.arange(16, dtype=jnp.int32)
    dense = jnp.sum(jnp.where(picked, gate_weights[:, :, None], 0.0), axis=1)
    everyone = lax.all_gather(dense.T, ("x", "zl"), axis=0, tiled=False)
    mine = lax.dynamic_index_in_dim(everyone, expert_num, axis=1, keepdims=False)
    mine = mine.reshape(4, 4, 64)
    mine = lax.dynamic_slice_in_dim(jnp.concatenate([mine, mine]), x, 4, axis=0)
    weight_a = mine[:, :, :32].transpose(1, 0, 2).reshape(512, 1)
    weight_b = mine[:, :, 32:].reshape(512, 1)
    up = jnp.transpose(up_weights[0], (1, 0, 2))
    down = down_weights[0]
    z_arr = z.astype(jnp.int32).reshape(1)

    b = gather_z(tokens[32:])
    a = gather_x(tokens[:32])
    b8 = jnp.concatenate([*b[:4], *b[4], *b[5:]])
    a4 = jnp.concatenate([a[0], a[1], *a[2], a[3]])
    b = gather_x(b8)
    a = gather_z(a4)
    pieces_b = [b[0], b[1], *b[2], b[3]]
    pieces_a = [*a[:4], *a[4], *a[5:]]

    yb = expert(z_arr, weight_b, pieces_b, up, down, plan_b(), [256] * 4, "experts_b")
    ya = expert(z_arr, weight_a, pieces_a, up, down, plan_a(), [128] * 8, "experts_a")

    sb = scatter_x(yb, yb[0]).astype(BF)
    sa = scatter_z(ya, ya[0]).astype(BF)
    sb = [sb[d * 32 : (d + 1) * 32] for d in range(8)]
    sa = [sa[d * 32 : (d + 1) * 32] for d in range(4)]
    out_b = scatter_z(sb, sb[0])
    out_a = scatter_x(sa, sa[0])
    return jnp.concatenate([out_a, out_b]).astype(BF)


def solution(mesh):
    fine = Mesh(mesh.devices.reshape(4, 4, 2, 4, 2), ("x", "zl", "zh", "y", "core"))
    rows = ("x", "zl", "y", "core")
    in_specs = (
        P(rows, "zh"),
        P(rows, None),
        P(rows, None),
        P(("x", "zl"), None, None, "zh"),
        P(("x", "zl"), "zh", None),
    )
    return jax.shard_map(
        local, mesh=fine, in_specs=in_specs, out_specs=P(rows, "zh"), check_vma=False
    )
```

```python
import functools

import jax
import jax.numpy as jnp
from jax import lax
from jax.experimental import pallas as pl
from jax.experimental.pallas import tpu as pltpu
from jax.sharding import Mesh
from jax.sharding import PartitionSpec as P

ZAX = ("zl", "zh")
BF = jnp.bfloat16
F32 = jnp.float32


def permute_x(v, step):
    return lax.ppermute(v, "x", [(i, (i + step) % 4) for i in range(4)])


def permute_z(v, step):
    index = lambda z: (z % 4) * 2 + z // 4
    return lax.ppermute(v, ZAX, [(index(z), index((z + step) % 8)) for z in range(8)])


def halves(v):
    n = v.shape[0] // 2
    return v[:n], v[n:]


def add(a, b):
    return (a.astype(F32) + b.astype(F32)).astype(BF)


def add_half(part, whole, which):
    w0, w1 = halves(whole)
    if which == 0:
        return jnp.concatenate([add(part, w0), w1])
    return jnp.concatenate([w0, add(part, w1)])


def fence(*values):
    return lax.optimization_barrier(values)


def weight_rows(dense):
    high = lax.reduce_precision(dense, 8, 7)
    rest = dense - high
    mid = lax.reduce_precision(rest, 8, 7)
    parts = jnp.stack([high, mid, rest - mid]).transpose(0, 2, 1).reshape(1, 1536)
    return jnp.pad(parts.astype(BF), ((0, 7), (0, 512)))


def weights_of(rows, expert_num):
    parts = rows[:, :1536].reshape(4, 3, 16, 32)
    parts = lax.dynamic_index_in_dim(parts, expert_num, axis=2, keepdims=False)
    return jnp.sum(parts.astype(F32), axis=1).reshape(128, 1)


def expert_kernel(in_plan, out_plan, n_in, n_out, z_ref, w_ref, *refs):
    ins = refs[:n_in]
    up_ref, down_ref = refs[n_in : n_in + 2]
    outs = refs[n_in + 2 : n_in + 2 + n_out]
    x_buf, up_buf, down_buf, hidden, y_buf, sem_x, sem_up, sem_down, sem_y = refs[n_in + 2 + n_out :]
    z = z_ref[0]

    def column(half):
        if isinstance(half, tuple):
            return pl.multiple_of(lax.div(lax.rem(z + half[1], 8), 4) * 2048, 2048)
        return half * 2048

    loads = [
        pltpu.make_async_copy(
            ins[ref].at[pl.ds(start, rows)],
            x_buf.at[pl.ds(row, rows), pl.ds(column(half), 2048)],
            sem_x,
        )
        for ref, start, rows, row, half in in_plan
    ]
    ups = [pltpu.make_async_copy(up_ref.at[n], up_buf.at[n], sem_up.at[n]) for n in range(4)]
    down_copy = pltpu.make_async_copy(down_ref, down_buf, sem_down)
    for c in loads:
        c.start()
    for c in ups:
        c.start()
    down_copy.start()
    for c in loads:
        c.wait()
    for n in range(4):
        ups[n].wait()
        both = jnp.dot(x_buf[...], up_buf[n], preferred_element_type=F32)
        gate, up = both[:, :128], both[:, 128:]
        hidden[:, n * 128 : (n + 1) * 128] = (gate / (1.0 + jnp.exp(-gate)) * up).astype(BF)
    down_copy.wait()
    w = w_ref[...]

    def down_step(n, _):
        at = pl.ds(pl.multiple_of(n * 256, 256), 256)
        y = jnp.dot(hidden[...], down_buf[:, at], preferred_element_type=F32)
        y_buf[:, at] = (y * w).astype(BF)
        return 0

    lax.fori_loop(0, 16, down_step, 0)
    stores = [
        pltpu.make_async_copy(
            y_buf.at[pl.ds(row, rows), pl.ds(column(half), 2048)],
            outs[ref].at[pl.ds(start, rows)],
            sem_y,
        )
        for ref, start, rows, row, half in out_plan
    ]
    for c in stores:
        c.start()
    for c in stores:
        c.wait()


def expert(z, weight, pieces, up, down, in_plan, out_plan, out_rows, name):
    n_in, n_out, rows = len(pieces), len(out_rows), weight.shape[0]
    any_spec = pl.BlockSpec(memory_space=pl.ANY)
    return pl.pallas_call(
        functools.partial(expert_kernel, in_plan, out_plan, n_in, n_out),
        out_shape=[jax.ShapeDtypeStruct((r, 2048), BF) for r in out_rows],
        in_specs=[
            pl.BlockSpec(memory_space=pltpu.SMEM),
            pl.BlockSpec(memory_space=pltpu.VMEM),
        ]
        + [any_spec] * (n_in + 2),
        out_specs=[any_spec] * n_out,
        scratch_shapes=[
            pltpu.VMEM((rows, 4096), BF),
            pltpu.VMEM((4, 4096, 256), BF),
            pltpu.VMEM((512, 4096), BF),
            pltpu.VMEM((rows, 512), BF),
            pltpu.VMEM((rows, 4096), BF),
            pltpu.SemaphoreType.DMA,
            pltpu.SemaphoreType.DMA((4,)),
            pltpu.SemaphoreType.DMA,
            pltpu.SemaphoreType.DMA,
        ],
        compiler_params=pltpu.CompilerParams(vmem_limit_bytes=32 << 20),
        name=name,
    )(z, weight, *pieces, up, down)


def local(tokens, expert_ids, gate_weights, up_weights, down_weights):
    x, zl, zh = lax.axis_index("x"), lax.axis_index("zl"), lax.axis_index("zh")
    z = zh * 4 + zl
    expert_num = x * 4 + zl
    z_arr = z.astype(jnp.int32).reshape(1)
    picked = expert_ids[:, :, None] == jnp.arange(16, dtype=jnp.int32)
    dense = jnp.sum(jnp.where(picked, gate_weights[:, :, None], 0.0), axis=1)

    a40 = jnp.concatenate([tokens[:32], weight_rows(dense[:32])])
    b40 = jnp.concatenate([tokens[32:], weight_rows(dense[32:])])
    b_all = lax.all_gather(b40, ("zh", "zl"), axis=0, tiled=False)
    a_by_x = [a40, permute_x(a40, -1), permute_x(a40, 2), permute_x(a40, 1)]
    a_tokens = jnp.concatenate([p[:32] for p in a_by_x])
    a_rows = jnp.concatenate([p[32:33] for p in a_by_x] + [jnp.zeros((4, 2048), BF)])
    a0 = jnp.concatenate([a_tokens, a_rows])
    left = permute_z(a_tokens, 1)
    right = permute_z(a0, -1)

    up = up_weights[0].reshape(4096, 2, 4, 128).transpose(2, 0, 1, 3).reshape(4, 4096, 256)
    down = down_weights[0]
    left, right, up = fence(left, right, up)

    lefts, rights = [left], [right]
    lefts.append(permute_z(lefts[-1], 1))
    rights.append(permute_z(rights[-1], -1))

    b0 = jnp.concatenate([b_all[:, :32].reshape(256, 2048), b_all[:4, 32], jnp.zeros((4, 2048), BF)])
    b_left = permute_x(b0, 1)
    b_right = permute_x(b0, -1)
    y_b0 = expert(
        z_arr, weights_of(b0[256:260], expert_num), [b0], up, down,
        [(0, 0, 128, 0, 0), (0, 128, 128, 0, 1)],
        [(0, 0, 128, 0, 0), (0, 128, 128, 0, 1)], [256], "experts_b0",
    )
    lefts.append(permute_z(lefts[-1], 1))
    rights.append(permute_z(rights[-1], -1))
    b_left, b_right, *y_b0 = fence(b_left, b_right, *y_b0)
    b_far0 = permute_x(jnp.concatenate([b_left[:128], b_left[256:]]), 1)
    b_far1 = permute_x(b_right[128:256], -1)
    a_far0 = permute_z(lefts[2][:64], 1)
    a_far1 = permute_z(rights[2][64:128], -1)

    w_a = [weights_of(p[128:132], expert_num) for p in [a0, *rights]]
    pairs = [(0, 1, 1), (1, 5, 1), (2, 2, 2), (3, 6, 2), (4, 3, 3), (5, 7, 3)]
    plan = [(ref, 0, 128, (p - 1) * 128, ("z", d)) for ref, d, p in pairs]
    y_a = expert(
        z_arr, jnp.concatenate(w_a[1:]),
        [rights[0], lefts[2], rights[1], lefts[1], rights[2], lefts[0]], up, down,
        plan, plan, [128] * 6, "experts_a123",
    )
    y_a1, y_a5, y_a2, y_a6, y_a3, y_a7 = y_a

    y_b2 = expert(
        z_arr, weights_of(b_far0[128:132], expert_num), [b_far0, b_far1], up, down,
        [(0, 0, 128, 0, 0), (1, 0, 128, 0, 1)],
        [(0, 0, 128, 0, 0), (1, 0, 128, 0, 1)], [128, 128], "experts_b2",
    )
    a_far0, a_far1, *y_b2 = fence(a_far0, a_far1, *y_b2)
    plan = [(0, 0, 128, 0, ("z", 0)), (1, 0, 64, 0, ("z", 4)), (2, 0, 64, 64, ("z", 4))]
    y_a0, y_a4a, y_a4b = expert(
        z_arr, w_a[0], [a_tokens, a_far0, a_far1], up, down,
        plan, plan, [128, 64, 64], "experts_a0",
    )
    b_left, b_right, y_a0, y_a4a, y_a4b = fence(b_left, b_right, y_a0, y_a4a, y_a4b)
    plan = [(r, h * 128, 128, r * 128, h) for r in range(2) for h in range(2)]
    y_b1, y_b3 = expert(
        z_arr,
        jnp.concatenate([weights_of(p[256:260], expert_num) for p in (b_right, b_left)]),
        [b_right, b_left], up, down, plan, plan, [256, 256], "experts_b13",
    )

    bl = permute_x(y_b2[0], 1)
    br = permute_x(y_b2[1], -1)
    al = permute_z(y_a4a, 1)
    ar = permute_z(y_a4b, -1)
    bl = permute_x(add_half(bl, y_b1, 0), 1)
    br = permute_x(add_half(br, y_b3, 1), -1)
    al = permute_z(add_half(al, y_a3, 0), 1)
    ar = permute_z(add_half(ar, y_a5, 1), -1)
    al = permute_z(add(al, y_a2), 1)
    ar = permute_z(add(ar, y_a6), -1)
    s_b = (y_b0[0].astype(F32) + bl.astype(F32) + br.astype(F32)).astype(BF)
    s_b = [
        lax.dynamic_slice_in_dim(s_b, lax.rem(z + d, 8) * 32, 32, axis=0) for d in range(8)
    ]
    al = permute_z(add(al, y_a1), 1)
    ar = permute_z(add(ar, y_a7), -1)
    bl = permute_z(s_b[4][:16], 1)
    br = permute_z(s_b[4][16:], -1)
    bl = permute_z(add_half(bl, s_b[3], 0), 1)
    br = permute_z(add_half(br, s_b[5], 1), -1)
    bl = permute_z(add(bl, s_b[2]), 1)
    br = permute_z(add(br, s_b[6]), -1)
    bl = permute_z(add(bl, s_b[1]), 1)
    br = permute_z(add(br, s_b[7]), -1)
    out_b = s_b[0].astype(F32) + bl.astype(F32) + br.astype(F32)

    s_a = y_a0.astype(F32) + al.astype(F32) + ar.astype(F32)
    far = [s_a[d * 32 : (d + 1) * 32].astype(BF) for d in range(1, 4)]
    got = [permute_x(far[0], 1), permute_x(far[1], 2), permute_x(far[2], 3)]
    out_a = s_a[:32] + got[0].astype(F32) + got[1].astype(F32) + got[2].astype(F32)
    return jnp.concatenate([out_a, out_b]).astype(BF)


def solution(mesh):
    fine = Mesh(mesh.devices.reshape(4, 4, 2, 4, 2), ("x", "zl", "zh", "y", "core"))
    rows = ("x", "zl", "y", "core")
    in_specs = (
        P(rows, "zh"),
        P(rows, None),
        P(rows, None),
        P(("x", "zl"), None, None, "zh"),
        P(("x", "zl"), "zh", None),
    )
    return jax.shard_map(
        local, mesh=fine, in_specs=in_specs, out_specs=P(rows, "zh"), check_vma=False
    )
```

```python
import functools

import jax
import jax.numpy as jnp
from jax import lax
from jax.experimental import pallas as pl
from jax.experimental.pallas import tpu as pltpu
from jax.sharding import Mesh
from jax.sharding import PartitionSpec as P

ZAX = ("zl", "zh")
BF = jnp.bfloat16
F32 = jnp.float32


def permute_x(v, step):
    return lax.ppermute(v, "x", [(i, (i + step) % 4) for i in range(4)])


def permute_z(v, step):
    index = lambda z: (z % 4) * 2 + z // 4
    return lax.ppermute(v, ZAX, [(index(z), index((z + step) % 8)) for z in range(8)])


def halves(v):
    n = v.shape[0] // 2
    return v[:n], v[n:]


def add(a, b):
    return (a.astype(F32) + b.astype(F32)).astype(BF)


def add_half(part, whole, which):
    w0, w1 = halves(whole)
    if which == 0:
        return jnp.concatenate([add(part, w0), w1])
    return jnp.concatenate([w0, add(part, w1)])


def fence(*values):
    return lax.optimization_barrier(values)


def weight_rows(dense):
    high = lax.reduce_precision(dense, 8, 7)
    rest = dense - high
    mid = lax.reduce_precision(rest, 8, 7)
    parts = jnp.stack([high, mid, rest - mid]).transpose(0, 2, 1).reshape(1, 1536)
    return jnp.broadcast_to(jnp.pad(parts.astype(BF), ((0, 0), (0, 512))), (8, 2048))


def pick_rows(blocks):
    row = lax.broadcasted_iota(jnp.int32, (8, 2048), 0)
    out = blocks[0]
    for r, block in enumerate(blocks[1:], 1):
        out = jnp.where(row == r, block, out)
    return out


def weights_of(rows, expert_num):
    parts = rows[:, :1536].reshape(4, 3, 16, 32)
    parts = lax.dynamic_index_in_dim(parts, expert_num, axis=2, keepdims=False)
    return jnp.sum(parts.astype(F32), axis=1).reshape(128, 1)


def expert_kernel(in_plan, out_plan, n_in, n_out, z_ref, w_ref, *refs):
    ins = refs[:n_in]
    up_ref, down_ref = refs[n_in : n_in + 2]
    outs = refs[n_in + 2 : n_in + 2 + n_out]
    x_buf, up_buf, down_buf, hidden, y_buf, sem_x, sem_up, sem_down, sem_y = refs[n_in + 2 + n_out :]
    z = z_ref[0]

    def column(half):
        if isinstance(half, tuple):
            return pl.multiple_of(lax.div(lax.rem(z + half[1], 8), 4) * 2048, 2048)
        return half * 2048

    loads = [
        pltpu.make_async_copy(
            ins[ref].at[pl.ds(start, rows)],
            x_buf.at[pl.ds(row, rows), pl.ds(column(half), 2048)],
            sem_x,
        )
        for ref, start, rows, row, half in in_plan
    ]
    ups = [
        [
            pltpu.make_async_copy(
                up_ref.at[g, :, pl.ds(n * 256, 256)],
                up_buf.at[n, :, pl.ds(g * 256, 256)],
                sem_up.at[n, g],
            )
            for g in range(2)
        ]
        for n in range(2)
    ]
    downs = [
        pltpu.make_async_copy(
            down_ref.at[:, pl.ds(n * 1024, 1024)], down_buf.at[:, pl.ds(n * 1024, 1024)], sem_down.at[n]
        )
        for n in range(4)
    ]
    for c in [*loads, *ups[0], *ups[1], *downs]:
        c.start()
    for c in loads:
        c.wait()
    for n in range(2):
        for c in ups[n]:
            c.wait()
        both = jnp.dot(x_buf[...], up_buf[n], preferred_element_type=F32)
        gate, up = both[:, :256], both[:, 256:]
        hidden[:, n * 256 : (n + 1) * 256] = (gate / (1.0 + jnp.exp(-gate)) * up).astype(BF)
    w = w_ref[...]
    for n in range(4):
        downs[n].wait()
        at = pl.ds(n * 1024, 1024)
        y = jnp.dot(hidden[...], down_buf[:, at], preferred_element_type=F32)
        y_buf[:, at] = (y * w).astype(BF)
    stores = [
        pltpu.make_async_copy(
            y_buf.at[pl.ds(row, rows), pl.ds(column(half), 2048)],
            outs[ref].at[pl.ds(start, rows)],
            sem_y,
        )
        for ref, start, rows, row, half in out_plan
    ]
    for c in stores:
        c.start()
    for c in stores:
        c.wait()


def expert(z, weight, pieces, up, down, in_plan, out_plan, out_rows, name):
    n_in, n_out, rows = len(pieces), len(out_rows), weight.shape[0]
    any_spec = pl.BlockSpec(memory_space=pl.ANY)
    vmem_spec = pl.BlockSpec(memory_space=pltpu.VMEM)
    return pl.pallas_call(
        functools.partial(expert_kernel, in_plan, out_plan, n_in, n_out),
        out_shape=[jax.ShapeDtypeStruct((r, 2048), BF) for r in out_rows],
        in_specs=[
            pl.BlockSpec(memory_space=pltpu.SMEM),
            vmem_spec,
        ]
        + [any_spec] * n_in
        + [any_spec] * 2,
        out_specs=[any_spec] * n_out,
        scratch_shapes=[
            pltpu.VMEM((rows, 4096), BF),
            pltpu.VMEM((2, 4096, 512), BF),
            pltpu.VMEM((512, 4096), BF),
            pltpu.VMEM((rows, 512), BF),
            pltpu.VMEM((rows, 4096), BF),
            pltpu.SemaphoreType.DMA,
            pltpu.SemaphoreType.DMA((2, 2)),
            pltpu.SemaphoreType.DMA((4,)),
            pltpu.SemaphoreType.DMA,
        ],
        compiler_params=pltpu.CompilerParams(vmem_limit_bytes=58 << 20),
        cost_estimate=pl.CostEstimate(
            flops=rows * 6 * 4096 * 512,
            transcendentals=rows * 512,
            bytes_accessed=12 * 2**20 + rows * 4 * 4096,
        ),
        name=name,
    )(z, weight, *pieces, up, down)


def local(tokens, expert_ids, gate_weights, up_weights, down_weights):
    x, zl, zh = lax.axis_index("x"), lax.axis_index("zl"), lax.axis_index("zh")
    z = zh * 4 + zl
    expert_num = x * 4 + zl
    z_arr = z.astype(jnp.int32).reshape(1)
    picked = expert_ids[:, :, None] == jnp.arange(16, dtype=jnp.int32)
    dense = jnp.sum(jnp.where(picked, gate_weights[:, :, None], 0.0), axis=1)

    a40 = jnp.concatenate([tokens[:32], weight_rows(dense[:32])])
    b40 = jnp.concatenate([tokens[32:], weight_rows(dense[32:])])
    b_all = lax.all_gather(b40, ("zh", "zl"), axis=0, tiled=False)
    up = jnp.transpose(up_weights[0], (1, 0, 2))
    down = down_weights[0]
    a1, a2, a3, up = fence(permute_x(a40, -1), permute_x(a40, 2), permute_x(a40, 1), up)
    a_by_x = [a40, a1, a2, a3]
    a_tokens = jnp.concatenate([p[:32] for p in a_by_x])
    a0 = jnp.concatenate([a_tokens, pick_rows([p[32:] for p in a_by_x])])
    left = permute_z(a_tokens, 1)
    right = permute_z(a0, -1)

    lefts, rights = [left], [right]
    lefts.append(permute_z(lefts[-1], 1))
    rights.append(permute_z(rights[-1], -1))

    b_rows = pick_rows([b_all[r, 32:] for r in range(8)])
    b0 = jnp.concatenate([b_all[:, :32].reshape(256, 2048), b_rows])
    b_left = permute_x(b0, 1)
    b_right = permute_x(b0, -1)
    y_b0 = expert(
        z_arr, weights_of(b0[256:260], expert_num), [b0], up, down,
        [(0, 0, 128, 0, 0), (0, 128, 128, 0, 1)],
        [(0, 0, 128, 0, 0), (0, 128, 128, 0, 1)], [256], "experts_b0",
    )
    lefts.append(permute_z(lefts[-1], 1))
    rights.append(permute_z(rights[-1], -1))
    b_left, b_right, *y_b0 = fence(b_left, b_right, *y_b0)
    b_far0 = permute_x(jnp.concatenate([b_left[:128], b_left[256:]]), 1)
    b_far1 = permute_x(b_right[128:256], -1)
    a_far0 = permute_z(lefts[2][:64], 1)
    a_far1 = permute_z(rights[2][64:128], -1)

    w_a = [weights_of(p[128:132], expert_num) for p in [a0, *rights]]
    pairs = [(0, 1, 1), (1, 5, 1), (2, 2, 2), (3, 6, 2), (4, 3, 3), (5, 7, 3)]
    plan = [(ref, 0, 128, (p - 1) * 128, ("z", d)) for ref, d, p in pairs]
    y_a = expert(
        z_arr, jnp.concatenate(w_a[1:]),
        [rights[0], lefts[2], rights[1], lefts[1], rights[2], lefts[0]], up, down,
        plan, plan, [128] * 6, "experts_a123",
    )
    b_far0, b_far1, *y_a = fence(b_far0, b_far1, *y_a)
    y_a1, y_a5, y_a2, y_a6, y_a3, y_a7 = y_a
    y_b2 = expert(
        z_arr, weights_of(b_far0[128:132], expert_num), [b_far0, b_far1], up, down,
        [(0, 0, 128, 0, 0), (1, 0, 128, 0, 1)],
        [(0, 0, 128, 0, 0), (1, 0, 128, 0, 1)], [128, 128], "experts_b2",
    )
    a_far0, a_far1, *y_b2 = fence(a_far0, a_far1, *y_b2)
    plan = [(0, 0, 128, 0, ("z", 0)), (1, 0, 64, 0, ("z", 4)), (2, 0, 64, 64, ("z", 4))]
    y_a0, y_a4a, y_a4b = expert(
        z_arr, w_a[0], [a_tokens, a_far0, a_far1], up, down,
        plan, plan, [128, 64, 64], "experts_a0",
    )
    b_left, b_right, y_a0, y_a4a, y_a4b = fence(b_left, b_right, y_a0, y_a4a, y_a4b)
    plan = [(r, h * 128, 128, r * 128, h) for r in range(2) for h in range(2)]
    y_b1, y_b3 = expert(
        z_arr,
        jnp.concatenate([weights_of(p[256:260], expert_num) for p in (b_right, b_left)]),
        [b_right, b_left], up, down, plan, plan, [256, 256], "experts_b13",
    )

    bl = permute_x(y_b2[0], 1)
    br = permute_x(y_b2[1], -1)
    al = permute_z(y_a4a, 1)
    ar = permute_z(y_a4b, -1)
    bl = permute_x(add_half(bl, y_b1, 0), 1)
    br = permute_x(add_half(br, y_b3, 1), -1)
    al = permute_z(add_half(al, y_a3, 0), 1)
    ar = permute_z(add_half(ar, y_a5, 1), -1)
    al = permute_z(add(al, y_a2), 1)
    ar = permute_z(add(ar, y_a6), -1)
    s_b = (y_b0[0].astype(F32) + bl.astype(F32) + br.astype(F32)).astype(BF)
    s_b = [
        lax.dynamic_slice_in_dim(s_b, lax.rem(z + d, 8) * 32, 32, axis=0) for d in range(8)
    ]
    al = permute_z(add(al, y_a1), 1)
    ar = permute_z(add(ar, y_a7), -1)
    bl = permute_z(s_b[4][:16], 1)
    br = permute_z(s_b[4][16:], -1)
    bl = permute_z(add_half(bl, s_b[3], 0), 1)
    br = permute_z(add_half(br, s_b[5], 1), -1)
    bl = permute_z(add(bl, s_b[2]), 1)
    br = permute_z(add(br, s_b[6]), -1)
    bl = permute_z(add(bl, s_b[1]), 1)
    br = permute_z(add(br, s_b[7]), -1)
    out_b = s_b[0].astype(F32) + bl.astype(F32) + br.astype(F32)

    s_a = y_a0.astype(F32) + al.astype(F32) + ar.astype(F32)
    far = [s_a[d * 32 : (d + 1) * 32].astype(BF) for d in range(1, 4)]
    got = [permute_x(far[0], 1), permute_x(far[1], 2), permute_x(far[2], 3)]
    out_a = s_a[:32] + got[0].astype(F32) + got[1].astype(F32) + got[2].astype(F32)
    return jnp.concatenate([out_a, out_b]).astype(BF)


def solution(mesh):
    fine = Mesh(mesh.devices.reshape(4, 4, 2, 4, 2), ("x", "zl", "zh", "y", "core"))
    rows = ("x", "zl", "y", "core")
    in_specs = (
        P(rows, "zh"),
        P(rows, None),
        P(rows, None),
        P(("x", "zl"), None, None, "zh"),
        P(("x", "zl"), "zh", None),
    )
    return jax.shard_map(
        local, mesh=fine, in_specs=in_specs, out_specs=P(rows, "zh"), check_vma=False
    )
```

```python
import functools

import jax
import jax.numpy as jnp
from jax import lax
from jax.experimental import pallas as pl
from jax.experimental.pallas import tpu as pltpu
from jax.sharding import Mesh
from jax.sharding import PartitionSpec as P

ZAX = ("zl", "zh")
BF = jnp.bfloat16
F32 = jnp.float32


def permute_x(v, step):
    return lax.ppermute(v, "x", [(i, (i + step) % 4) for i in range(4)])


def permute_z(v, step):
    index = lambda z: (z % 4) * 2 + z // 4
    return lax.ppermute(v, ZAX, [(index(z), index((z + step) % 8)) for z in range(8)])


def halves(v):
    n = v.shape[0] // 2
    return v[:n], v[n:]


def add(a, b):
    return (a.astype(F32) + b.astype(F32)).astype(BF)


def add_half(part, whole, which):
    w0, w1 = halves(whole)
    if which == 0:
        return jnp.concatenate([add(part, w0), w1])
    return jnp.concatenate([w0, add(part, w1)])


def fence(*values):
    return lax.optimization_barrier(values)


def weight_rows(dense):
    high = lax.reduce_precision(dense, 8, 7)
    rest = dense - high
    mid = lax.reduce_precision(rest, 8, 7)
    parts = jnp.stack([high, mid, rest - mid]).transpose(0, 2, 1).reshape(1, 1536)
    return jnp.broadcast_to(jnp.pad(parts.astype(BF), ((0, 0), (0, 512))), (8, 2048))


def pick_rows(blocks):
    row = lax.broadcasted_iota(jnp.int32, (8, 2048), 0)
    out = blocks[0]
    for r, block in enumerate(blocks[1:], 1):
        out = jnp.where(row == r, block, out)
    return out


def scatter_x_ring(y):
    l = permute_x(halves(y[2])[0], 1)
    r = permute_x(halves(y[2])[1], -1)
    l = permute_x(add_half(l, y[1], 0), 1)
    r = permute_x(add_half(r, y[3], 1), -1)
    return y[0].astype(F32) + l.astype(F32) + r.astype(F32)


def scatter_z_ring(y):
    l = permute_z(halves(y[4])[0], 1)
    r = permute_z(halves(y[4])[1], -1)
    l = permute_z(add_half(l, y[3], 0), 1)
    r = permute_z(add_half(r, y[5], 1), -1)
    l = permute_z(add(l, y[2]), 1)
    r = permute_z(add(r, y[6]), -1)
    l = permute_z(add(l, y[1]), 1)
    r = permute_z(add(r, y[7]), -1)
    return y[0].astype(F32) + l.astype(F32) + r.astype(F32)


def expert_kernel(loads, blocks, stores, n_in, n_out, place_ref, *refs):
    ins = refs[:n_in]
    up_ref, down_ref = refs[n_in : n_in + 2]
    outs = refs[n_in + 2 : n_in + 2 + n_out]
    x_buf, up_buf, down_buf, hidden, y_buf, rows_buf, w_buf, sem_x, sem_up, sem_down, sem_y = refs[n_in + 2 + n_out :]
    z, expert_num = place_ref[0], place_ref[1]

    def half_of(d):
        return lax.div(lax.rem(z + d, 8), 4)

    in_copies = [
        pltpu.make_async_copy(
            ins[ref].at[pl.ds(start, rows)],
            x_buf.at[pl.ds(row, rows), pl.ds(pl.multiple_of(half_of(d) * 2048, 2048), 2048)],
            sem_x,
        )
        for ref, start, rows, row, d in loads
    ] + [
        pltpu.make_async_copy(ins[ref].at[pl.ds(start, 8)], rows_buf.at[i], sem_x)
        for i, (ref, start) in enumerate(blocks)
    ]
    ups = [
        [
            pltpu.make_async_copy(
                up_ref.at[g, :, pl.ds(n * 256, 256)],
                up_buf.at[n, :, pl.ds(g * 256, 256)],
                sem_up.at[n, g],
            )
            for g in range(2)
        ]
        for n in range(2)
    ]
    downs = [
        pltpu.make_async_copy(
            down_ref.at[:, pl.ds(h * 2048, 2048)], down_buf.at[:, pl.ds(h * 2048, 2048)], sem_down.at[h]
        )
        for h in range(2)
    ]
    for c in [*in_copies, *ups[0], *ups[1], *downs]:
        c.start()
    for c in in_copies:
        c.wait()

    group = pl.multiple_of(lax.div(expert_num, 4) * 128, 128)
    lane = lax.broadcasted_iota(jnp.int32, (32, 128), 1)
    token = lax.broadcasted_iota(jnp.int32, (32, 128), 0)
    mine = lane == lax.rem(expert_num, 4) * 32 + token
    for i in range(len(blocks)):
        parts = [rows_buf[i, :, pl.ds(group + part * 512, 128)].astype(F32) for part in range(3)]
        total = parts[0] + parts[1] + parts[2]
        for j in range(4):
            picked = jnp.where(mine, jnp.broadcast_to(total[j : j + 1], (32, 128)), 0.0)
            w_buf[i * 128 + j * 32 : i * 128 + (j + 1) * 32, :] = jnp.broadcast_to(
                jnp.sum(picked, axis=1, keepdims=True), (32, 128)
            )

    for n in range(2):
        for c in ups[n]:
            c.wait()
        both = jnp.dot(x_buf[...], up_buf[n], preferred_element_type=F32)
        gate, up = both[:, :256], both[:, 256:]
        hidden[:, n * 256 : (n + 1) * 256] = (gate / (1.0 + jnp.exp(-gate)) * up).astype(BF)
    w = w_buf[:, :1]
    out_copies = []
    for h in range(2):
        downs[h].wait()

        def down_step(n, _):
            at = pl.ds(pl.multiple_of(h * 2048 + n * 512, 512), 512)
            y = jnp.dot(hidden[...], down_buf[:, at], preferred_element_type=F32)
            y_buf[:, at] = (y * w).astype(BF)
            return 0

        lax.fori_loop(0, 4, down_step, 0)
        for ref, start, rows, row, p in stores:
            d = p + 4 * lax.rem(half_of(p) + h, 2)
            c = pltpu.make_async_copy(
                y_buf.at[pl.ds(row, rows), pl.ds(h * 2048, 2048)],
                outs[ref].at[pl.ds(pl.multiple_of(start + d * rows, rows), rows)],
                sem_y,
            )
            c.start()
            out_copies.append(c)
    for c in out_copies:
        c.wait()


def expert(place, pieces, up, down, loads, blocks, stores, out_rows, name):
    n_in, n_out, rows = len(pieces), len(out_rows), len(blocks) * 128
    any_spec = pl.BlockSpec(memory_space=pl.ANY)
    return pl.pallas_call(
        functools.partial(expert_kernel, loads, blocks, stores, n_in, n_out),
        out_shape=[jax.ShapeDtypeStruct((r, 2048), BF) for r in out_rows],
        in_specs=[pl.BlockSpec(memory_space=pltpu.SMEM)] + [any_spec] * (n_in + 2),
        out_specs=[any_spec] * n_out,
        scratch_shapes=[
            pltpu.VMEM((rows, 4096), BF),
            pltpu.VMEM((2, 4096, 512), BF),
            pltpu.VMEM((512, 4096), BF),
            pltpu.VMEM((rows, 512), BF),
            pltpu.VMEM((rows, 4096), BF),
            pltpu.VMEM((len(blocks), 8, 2048), BF),
            pltpu.VMEM((rows, 128), F32),
            pltpu.SemaphoreType.DMA,
            pltpu.SemaphoreType.DMA((2, 2)),
            pltpu.SemaphoreType.DMA((2,)),
            pltpu.SemaphoreType.DMA,
        ],
        compiler_params=pltpu.CompilerParams(vmem_limit_bytes=48 << 20),
        cost_estimate=pl.CostEstimate(
            flops=rows * 6 * 4096 * 512,
            transcendentals=rows * 512,
            bytes_accessed=12 * 2**20 + rows * 4 * 4096,
        ),
        name=name,
    )(place, *pieces, up, down)


def local(tokens, expert_ids, gate_weights, up_weights, down_weights):
    x, zl, zh = lax.axis_index("x"), lax.axis_index("zl"), lax.axis_index("zh")
    place = jnp.stack([zh * 4 + zl, x * 4 + zl]).astype(jnp.int32)
    picked = expert_ids[:, :, None] == jnp.arange(16, dtype=jnp.int32)
    dense = jnp.sum(jnp.where(picked, gate_weights[:, :, None], 0.0), axis=1)
    down = down_weights[0]

    b40 = jnp.concatenate([tokens[32:], weight_rows(dense[32:])])
    a40 = jnp.concatenate([tokens[:32], weight_rows(dense[:32])])
    bl, br = [tokens[32:]], [b40]
    bl.append(permute_z(bl[0], 1))
    br.append(permute_z(br[0], -1))
    a1, a2, a3, bl[1], br[1] = fence(permute_x(a40, -1), permute_x(a40, 2), permute_x(a40, 1), bl[1], br[1])
    a_by_x = [a40, a1, a2, a3]
    a_tokens = jnp.concatenate([v[:32] for v in a_by_x])
    a0 = jnp.concatenate([a_tokens, pick_rows([v[32:] for v in a_by_x])])
    al = [a_tokens, permute_z(a_tokens, 1)]
    ar = [a0, permute_z(a0, -1)]
    bl.append(permute_z(bl[1], 1))
    br.append(permute_z(br[1], -1))
    al[1], ar[1], bl[2], br[2] = fence(al[1], ar[1], bl[2], br[2])
    bl.append(permute_z(bl[2], 1))
    br.append(permute_z(br[2], -1))
    b_far0 = permute_z(bl[3][:16], 1)
    b_far1 = permute_z(br[3][16:32], -1)

    up = jnp.transpose(up_weights[0], (1, 0, 2))
    for step in (1, 2):
        al.append(permute_z(al[-1], 1))
        ar.append(permute_z(ar[-1], -1))
        if step == 1:
            al[2], ar[2], up = fence(al[2], ar[2], up)
    a_far0 = permute_z(al[3][:64], 1)
    a_far1 = permute_z(ar[3][64:128], -1)

    b_rows = pick_rows([v[32:] for v in br])
    b0 = jnp.concatenate([v[:32] for v in br] + [b_far0, b_far1, bl[3], bl[2], bl[1], b_rows])
    b_left = permute_x(b0, 1)
    b_right = permute_x(b0, -1)
    b_far0 = permute_x(jnp.concatenate([b_left[:128], b_left[256:]]), 1)
    b_far1 = permute_x(b_right[128:256], -1)

    def plan_b(sources):
        loads, stores = [], []
        for i, (near, far) in enumerate(sources):
            for q in range(4):
                loads.append((near[0], near[1] + q * 32, 32, i * 128 + q * 32, q))
                loads.append((far[0], far[1] + q * 32, 32, i * 128 + q * 32, q + 4))
                stores.append((i, 0, 32, i * 128 + q * 32, q))
        return loads, stores

    loads, stores = plan_b([((i, 0), (i, 128)) for i in range(3)])
    y_b0, y_b1, y_b3 = expert(
        place, [b0, b_right, b_left], up, down, loads, [(i, 256) for i in range(3)], stores, [256] * 3, "experts_b013"
    )
    b_far0, b_far1, y_b0, y_b1, y_b3 = fence(b_far0, b_far1, y_b0, y_b1, y_b3)
    loads, stores = plan_b([((0, 0), (1, 0))])
    (y_b2,) = expert(place, [b_far0, b_far1], up, down, loads, [(0, 128)], stores, [256], "experts_b2")

    a_far0, a_far1, y_b2 = fence(a_far0, a_far1, y_b2)
    pieces = [*ar, a_far0, a_far1, al[3], al[2], al[1]]
    loads = [(d, 0, 128, d * 128, d) for d in range(4)]
    loads += [(4, 0, 64, 0, 4), (5, 0, 64, 64, 4)]
    loads += [(d + 1, 0, 128, (d - 4) * 128, d) for d in range(5, 8)]
    stores = [(0, 0, 128, q * 128, q) for q in range(4)]
    (y_a,) = expert(place, pieces, up, down, loads, [(d, 128) for d in range(4)], stores, [1024], "experts_a")
    y_a = [y_a[d * 128 : (d + 1) * 128] for d in range(8)]

    out_b = scatter_x_ring([y_b0, y_b1, y_b2, y_b3]).astype(BF)
    s_a = scatter_z_ring(y_a)
    out_b = scatter_z_ring([out_b[d * 32 : (d + 1) * 32] for d in range(8)])
    far = [s_a[d * 32 : (d + 1) * 32].astype(BF) for d in range(1, 4)]
    got = [permute_x(far[0], 1), permute_x(far[1], 2), permute_x(far[2], 3)]
    out_a = s_a[:32] + got[0].astype(F32) + got[1].astype(F32) + got[2].astype(F32)
    return jnp.concatenate([out_a, out_b]).astype(BF)


def solution(mesh):
    fine = Mesh(mesh.devices.reshape(4, 4, 2, 4, 2), ("x", "zl", "zh", "y", "core"))
    rows = ("x", "zl", "y", "core")
    in_specs = (
        P(rows, "zh"),
        P(rows, None),
        P(rows, None),
        P(("x", "zl"), None, None, "zh"),
        P(("x", "zl"), "zh", None),
    )
    return jax.shard_map(
        local, mesh=fine, in_specs=in_specs, out_specs=P(rows, "zh"), check_vma=False
    )
```

```python
import functools

import jax
import jax.numpy as jnp
from jax import lax
from jax.experimental import pallas as pl
from jax.experimental.pallas import tpu as pltpu
from jax.sharding import Mesh
from jax.sharding import PartitionSpec as P

ZAX = ("zl", "zh")
BF = jnp.bfloat16
F32 = jnp.float32


def permute_x(v, step):
    return lax.ppermute(v, "x", [(i, (i + step) % 4) for i in range(4)])


def permute_z(v, step):
    index = lambda z: (z % 4) * 2 + z // 4
    return lax.ppermute(v, ZAX, [(index(z), index((z + step) % 8)) for z in range(8)])


def halves(v):
    n = v.shape[0] // 2
    return v[:n], v[n:]


def add(a, b):
    return (a.astype(F32) + b.astype(F32)).astype(BF)


def add_half(part, whole, which):
    w0, w1 = halves(whole)
    if which == 0:
        return jnp.concatenate([add(part, w0), w1])
    return jnp.concatenate([w0, add(part, w1)])


def fence(*values):
    return lax.optimization_barrier(values)


def weight_rows(dense):
    high = lax.reduce_precision(dense, 8, 7)
    rest = dense - high
    mid = lax.reduce_precision(rest, 8, 7)
    parts = jnp.stack([high, mid, rest - mid]).transpose(0, 2, 1).reshape(1, 1536)
    return jnp.broadcast_to(jnp.pad(parts.astype(BF), ((0, 0), (0, 512))), (8, 2048))


def pick_rows(blocks):
    row = lax.broadcasted_iota(jnp.int32, (8, 2048), 0)
    out = blocks[0]
    for r, block in enumerate(blocks[1:], 1):
        out = jnp.where(row == r, block, out)
    return out


def scatter_x_ring(y):
    l = permute_x(halves(y[2])[0], 1)
    r = permute_x(halves(y[2])[1], -1)
    l = permute_x(add_half(l, y[1], 0), 1)
    r = permute_x(add_half(r, y[3], 1), -1)
    return y[0].astype(F32) + l.astype(F32) + r.astype(F32)


def scatter_z_ring(y, split):
    if split:
        l = permute_z(halves(y[4])[0], 1)
        r = permute_z(halves(y[4])[1], -1)
        l = permute_z(add_half(l, y[3], 0), 1)
        r = permute_z(add_half(r, y[5], 1), -1)
    else:
        l = permute_z(y[4], 1)
        r = permute_z(y[5], -1)
        l = permute_z(add(l, y[3]), 1)
    l = permute_z(add(l, y[2]), 1)
    r = permute_z(add(r, y[6]), -1)
    l = permute_z(add(l, y[1]), 1)
    r = permute_z(add(r, y[7]), -1)
    return y[0].astype(F32) + l.astype(F32) + r.astype(F32)


def expert_kernel(loads, blocks, stores, n_in, n_out, place_ref, *refs):
    ins = refs[:n_in]
    up_ref, down_ref = refs[n_in : n_in + 2]
    outs = refs[n_in + 2 : n_in + 2 + n_out]
    x_buf, up_buf, down_buf, hidden, y_buf, rows_buf, w_buf, sem_x, sem_up, sem_down, sem_y = refs[n_in + 2 + n_out :]
    z, expert_num = place_ref[0], place_ref[1]

    def half_of(d):
        return lax.div(lax.rem(z + d, 8), 4)

    in_copies = [
        pltpu.make_async_copy(
            ins[ref].at[pl.ds(start, rows)],
            x_buf.at[pl.ds(row, rows), pl.ds(pl.multiple_of(half_of(d) * 2048, 2048), 2048)],
            sem_x,
        )
        for ref, start, rows, row, d in loads
    ] + [
        pltpu.make_async_copy(ins[ref].at[pl.ds(start, 8)], rows_buf.at[i], sem_x)
        for i, (ref, start) in enumerate(blocks)
    ]
    ups = [
        [
            pltpu.make_async_copy(
                up_ref.at[g, :, pl.ds(n * 256, 256)],
                up_buf.at[n, :, pl.ds(g * 256, 256)],
                sem_up.at[n, g],
            )
            for g in range(2)
        ]
        for n in range(2)
    ]
    downs = [
        pltpu.make_async_copy(
            down_ref.at[:, pl.ds(h * 2048, 2048)], down_buf.at[:, pl.ds(h * 2048, 2048)], sem_down.at[h]
        )
        for h in range(2)
    ]
    for c in [*in_copies, *ups[0], *ups[1], *downs]:
        c.start()
    for c in in_copies:
        c.wait()

    group = pl.multiple_of(lax.div(expert_num, 4) * 128, 128)
    lane = lax.broadcasted_iota(jnp.int32, (32, 128), 1)
    token = lax.broadcasted_iota(jnp.int32, (32, 128), 0)
    mine = lane == lax.rem(expert_num, 4) * 32 + token
    for i in range(len(blocks)):
        parts = [rows_buf[i, :, pl.ds(group + part * 512, 128)].astype(F32) for part in range(3)]
        total = parts[0] + parts[1] + parts[2]
        for j in range(4):
            picked = jnp.where(mine, jnp.broadcast_to(total[j : j + 1], (32, 128)), 0.0)
            w_buf[i * 128 + j * 32 : i * 128 + (j + 1) * 32, :] = jnp.broadcast_to(
                jnp.sum(picked, axis=1, keepdims=True), (32, 128)
            )

    def up_step(n, _):
        for g in range(2):
            pltpu.make_async_copy(
                up_ref.at[g, :, pl.ds(0, 256)], up_buf.at[n, :, pl.ds(g * 256, 256)], sem_up.at[n, g]
            ).wait()
        both = jnp.dot(x_buf[...], up_buf[n], preferred_element_type=F32)
        gate, up = both[:, :256], both[:, 256:]
        at = pl.ds(pl.multiple_of(n * 256, 256), 256)
        hidden[:, at] = (gate / (1.0 + jnp.exp(-gate)) * up).astype(BF)
        return 0

    lax.fori_loop(0, 2, up_step, 0)
    w = w_buf[:, :1]
    out_copies = []
    for h in range(2):
        downs[h].wait()

        def down_step(n, _):
            at = pl.ds(pl.multiple_of(h * 2048 + n * 512, 512), 512)
            y = jnp.dot(hidden[...], down_buf[:, at], preferred_element_type=F32)
            y_buf[:, at] = (y * w).astype(BF)
            return 0

        lax.fori_loop(0, 4, down_step, 0)
        for ref, start, rows, row, p in stores:
            d = p + 4 * lax.rem(half_of(p) + h, 2)
            c = pltpu.make_async_copy(
                y_buf.at[pl.ds(row, rows), pl.ds(h * 2048, 2048)],
                outs[ref].at[pl.ds(pl.multiple_of(start + d * rows, rows), rows)],
                sem_y,
            )
            c.start()
            out_copies.append(c)
    for c in out_copies:
        c.wait()


def expert(place, pieces, up, down, loads, blocks, stores, out_rows, name):
    n_in, n_out, rows = len(pieces), len(out_rows), len(blocks) * 128
    any_spec = pl.BlockSpec(memory_space=pl.ANY)
    return pl.pallas_call(
        functools.partial(expert_kernel, loads, blocks, stores, n_in, n_out),
        out_shape=[jax.ShapeDtypeStruct((r, 2048), BF) for r in out_rows],
        in_specs=[pl.BlockSpec(memory_space=pltpu.SMEM)] + [any_spec] * (n_in + 2),
        out_specs=[any_spec] * n_out,
        scratch_shapes=[
            pltpu.VMEM((rows, 4096), BF),
            pltpu.VMEM((2, 4096, 512), BF),
            pltpu.VMEM((512, 4096), BF),
            pltpu.VMEM((rows, 512), BF),
            pltpu.VMEM((rows, 4096), BF),
            pltpu.VMEM((len(blocks), 8, 2048), BF),
            pltpu.VMEM((rows, 128), F32),
            pltpu.SemaphoreType.DMA,
            pltpu.SemaphoreType.DMA((2, 2)),
            pltpu.SemaphoreType.DMA((2,)),
            pltpu.SemaphoreType.DMA,
        ],
        compiler_params=pltpu.CompilerParams(vmem_limit_bytes=48 << 20),
        cost_estimate=pl.CostEstimate(
            flops=rows * 6 * 4096 * 512,
            transcendentals=rows * 512,
            bytes_accessed=12 * 2**20 + rows * 4 * 4096,
        ),
        name=name,
    )(place, *pieces, up, down)


def local(tokens, expert_ids, gate_weights, up_weights, down_weights):
    x, zl, zh = lax.axis_index("x"), lax.axis_index("zl"), lax.axis_index("zh")
    place = jnp.stack([zh * 4 + zl, x * 4 + zl]).astype(jnp.int32)
    picked = expert_ids[:, :, None] == jnp.arange(16, dtype=jnp.int32)
    dense = jnp.sum(jnp.where(picked, gate_weights[:, :, None], 0.0), axis=1)
    down = down_weights[0]

    b40 = jnp.concatenate([tokens[32:], weight_rows(dense[32:])])
    a40 = jnp.concatenate([tokens[:32], weight_rows(dense[:32])])
    bl, br = [tokens[32:]], [b40]
    for step in range(3):
        bl.append(permute_z(bl[-1], 1))
        br.append(permute_z(br[-1], -1))
        if step == 0:
            a1, a2, a3 = permute_x(a40, -1), permute_x(a40, 2), permute_x(a40, 1)
    b_far = permute_z(bl[3], 1)

    a_by_x = [a40, a1, a2, a3]
    a_tokens = jnp.concatenate([v[:32] for v in a_by_x])
    a0 = jnp.concatenate([a_tokens, pick_rows([v[32:] for v in a_by_x])])
    al, ar = [a_tokens], [a0]
    up = jnp.transpose(up_weights[0], (1, 0, 2))
    for step in range(3):
        al.append(permute_z(al[-1], 1))
        ar.append(permute_z(ar[-1], -1))
        if step == 1:
            al[2], ar[2], up = fence(al[2], ar[2], up)
    a_far0 = permute_z(al[3][:64], 1)
    a_far1 = permute_z(ar[3][64:128], -1)

    b_rows = pick_rows([v[32:] for v in br])
    b0 = jnp.concatenate([v[:32] for v in br] + [b_far, bl[3], bl[2], bl[1], b_rows])
    b_left = permute_x(b0, 1)
    b_right = permute_x(b0, -1)
    b_far0 = permute_x(jnp.concatenate([b_left[:128], b_left[256:]]), 1)
    b_far1 = permute_x(b_right[128:256], -1)

    def plan_b(sources):
        loads, stores = [], []
        for i, (near, far) in enumerate(sources):
            for q in range(4):
                loads.append((near[0], near[1] + q * 32, 32, i * 128 + q * 32, q))
                loads.append((far[0], far[1] + q * 32, 32, i * 128 + q * 32, q + 4))
                stores.append((i, 0, 32, i * 128 + q * 32, q))
        return loads, stores

    loads, stores = plan_b([((i, 0), (i, 128)) for i in range(3)])
    y_b0, y_b1, y_b3 = expert(
        place, [b0, b_right, b_left], up, down, loads, [(i, 256) for i in range(3)], stores, [256] * 3, "experts_b013"
    )
    b_far0, b_far1, y_b0, y_b1, y_b3 = fence(b_far0, b_far1, y_b0, y_b1, y_b3)
    loads, stores = plan_b([((0, 0), (1, 0))])
    (y_b2,) = expert(place, [b_far0, b_far1], up, down, loads, [(0, 128)], stores, [256], "experts_b2")

    a_far0, a_far1, y_b2 = fence(a_far0, a_far1, y_b2)
    pieces = [*ar, a_far0, a_far1, al[3], al[2], al[1]]
    loads = [(d, 0, 128, d * 128, d) for d in range(4)]
    loads += [(4, 0, 64, 0, 4), (5, 0, 64, 64, 4)]
    loads += [(d + 1, 0, 128, (d - 4) * 128, d) for d in range(5, 8)]
    stores = [(0, 0, 128, q * 128, q) for q in range(4)]
    (y_a,) = expert(place, pieces, up, down, loads, [(d, 128) for d in range(4)], stores, [1024], "experts_a")
    y_a = [y_a[d * 128 : (d + 1) * 128] for d in range(8)]

    out_b = scatter_x_ring([y_b0, y_b1, y_b2, y_b3]).astype(BF)
    s_a = scatter_z_ring(y_a, True)
    out_b = scatter_z_ring([out_b[d * 32 : (d + 1) * 32] for d in range(8)], False)
    far = [s_a[d * 32 : (d + 1) * 32].astype(BF) for d in range(1, 4)]
    got = [permute_x(far[0], 1), permute_x(far[1], 2), permute_x(far[2], 3)]
    out_a = s_a[:32] + got[0].astype(F32) + got[1].astype(F32) + got[2].astype(F32)
    return jnp.concatenate([out_a, out_b]).astype(BF)


def solution(mesh):
    fine = Mesh(mesh.devices.reshape(4, 4, 2, 4, 2), ("x", "zl", "zh", "y", "core"))
    rows = ("x", "zl", "y", "core")
    in_specs = (
        P(rows, "zh"),
        P(rows, None),
        P(rows, None),
        P(("x", "zl"), None, None, "zh"),
        P(("x", "zl"), "zh", None),
    )
    return jax.shard_map(
        local, mesh=fine, in_specs=in_specs, out_specs=P(rows, "zh"), check_vma=False
    )
```

```python
import functools

import jax
import jax.numpy as jnp
from jax import lax
from jax.experimental import pallas as pl
from jax.experimental.pallas import tpu as pltpu
from jax.sharding import Mesh
from jax.sharding import PartitionSpec as P

ZAX = ("zl", "zh")
BF = jnp.bfloat16
F32 = jnp.float32


def permute_x(v, step):
    return lax.ppermute(v, "x", [(i, (i + step) % 4) for i in range(4)])


def permute_z(v, step):
    index = lambda z: (z % 4) * 2 + z // 4
    return lax.ppermute(v, ZAX, [(index(z), index((z + step) % 8)) for z in range(8)])


def halves(v):
    n = v.shape[0] // 2
    return v[:n], v[n:]


def add(a, b):
    return (a.astype(F32) + b.astype(F32)).astype(BF)


def add_half(part, whole, which):
    w0, w1 = halves(whole)
    if which == 0:
        return jnp.concatenate([add(part, w0), w1])
    return jnp.concatenate([w0, add(part, w1)])


def fence(*values):
    return lax.optimization_barrier(values)


def weight_rows(dense):
    high = lax.reduce_precision(dense, 8, 7)
    rest = dense - high
    mid = lax.reduce_precision(rest, 8, 7)
    parts = jnp.stack([high, mid, rest - mid]).transpose(0, 2, 1).reshape(1, 1536)
    return jnp.broadcast_to(jnp.pad(parts.astype(BF), ((0, 0), (0, 512))), (8, 2048))


def pick_rows(blocks):
    row = lax.broadcasted_iota(jnp.int32, (8, 2048), 0)
    out = blocks[0]
    for r, block in enumerate(blocks[1:], 1):
        out = jnp.where(row == r, block, out)
    return out


def expert_kernel(loads, blocks, stores, n_in, n_out, place_ref, *refs):
    ins = refs[:n_in]
    up_ref, down_ref = refs[n_in : n_in + 2]
    outs = refs[n_in + 2 : n_in + 2 + n_out]
    x_buf, up_buf, down_buf, hidden, y_buf, rows_buf, w_buf, sem_x, sem_up, sem_down, sem_y = refs[n_in + 2 + n_out :]
    z, expert_num = place_ref[0], place_ref[1]

    def half_of(d):
        return lax.div(lax.rem(z + d, 8), 4)

    in_copies = [
        pltpu.make_async_copy(
            ins[ref].at[pl.ds(start, rows)],
            x_buf.at[pl.ds(row, rows), pl.ds(pl.multiple_of(half_of(d) * 2048, 2048), 2048)],
            sem_x,
        )
        for ref, start, rows, row, d in loads
    ] + [
        pltpu.make_async_copy(ins[ref].at[pl.ds(start, 8)], rows_buf.at[i], sem_x)
        for i, (ref, start) in enumerate(blocks)
    ]
    ups = [
        [
            pltpu.make_async_copy(
                up_ref.at[g, :, pl.ds(n * 256, 256)],
                up_buf.at[n, :, pl.ds(g * 256, 256)],
                sem_up.at[n, g],
            )
            for g in range(2)
        ]
        for n in range(2)
    ]
    downs = [
        pltpu.make_async_copy(
            down_ref.at[:, pl.ds(h * 2048, 2048)], down_buf.at[:, pl.ds(h * 2048, 2048)], sem_down.at[h]
        )
        for h in range(2)
    ]
    for c in [*in_copies, *ups[0], *ups[1], *downs]:
        c.start()
    for c in in_copies:
        c.wait()

    group = pl.multiple_of(lax.div(expert_num, 4) * 128, 128)
    lane = lax.broadcasted_iota(jnp.int32, (32, 128), 1)
    token = lax.broadcasted_iota(jnp.int32, (32, 128), 0)
    mine = lane == lax.rem(expert_num, 4) * 32 + token
    for i in range(len(blocks)):
        parts = [rows_buf[i, :, pl.ds(group + part * 512, 128)].astype(F32) for part in range(3)]
        total = parts[0] + parts[1] + parts[2]
        for j in range(4):
            picked = jnp.where(mine, jnp.broadcast_to(total[j : j + 1], (32, 128)), 0.0)
            w_buf[i * 128 + j * 32 : i * 128 + (j + 1) * 32, :] = jnp.broadcast_to(
                jnp.sum(picked, axis=1, keepdims=True), (32, 128)
            )

    for n in range(2):
        for c in ups[n]:
            c.wait()
        both = jnp.dot(x_buf[...], up_buf[n], preferred_element_type=F32)
        gate, up = both[:, :256], both[:, 256:]
        hidden[:, n * 256 : (n + 1) * 256] = (gate / (1.0 + jnp.exp(-gate)) * up).astype(BF)
    w = w_buf[:, :1]
    out_copies = []
    for h in range(2):
        downs[h].wait()
        for n in range(2):
            at = pl.ds(h * 2048 + n * 1024, 1024)
            y = jnp.dot(hidden[...], down_buf[:, at], preferred_element_type=F32)
            y_buf[:, at] = (y * w).astype(BF)
        for ref, start, rows, row, p in stores:
            d = p + 4 * lax.rem(half_of(p) + h, 2)
            c = pltpu.make_async_copy(
                y_buf.at[pl.ds(row, rows), pl.ds(h * 2048, 2048)],
                outs[ref].at[pl.ds(pl.multiple_of(start + d * rows, rows), rows)],
                sem_y,
            )
            c.start()
            out_copies.append(c)
    for c in out_copies:
        c.wait()


def expert(place, pieces, up, down, loads, blocks, stores, out_rows, name):
    n_in, n_out, rows = len(pieces), len(out_rows), len(blocks) * 128
    any_spec = pl.BlockSpec(memory_space=pl.ANY)
    return pl.pallas_call(
        functools.partial(expert_kernel, loads, blocks, stores, n_in, n_out),
        out_shape=[jax.ShapeDtypeStruct((r, 2048), BF) for r in out_rows],
        in_specs=[pl.BlockSpec(memory_space=pltpu.SMEM)] + [any_spec] * (n_in + 2),
        out_specs=[any_spec] * n_out,
        scratch_shapes=[
            pltpu.VMEM((rows, 4096), BF),
            pltpu.VMEM((2, 4096, 512), BF),
            pltpu.VMEM((512, 4096), BF),
            pltpu.VMEM((rows, 512), BF),
            pltpu.VMEM((rows, 4096), BF),
            pltpu.VMEM((len(blocks), 8, 2048), BF),
            pltpu.VMEM((rows, 128), F32),
            pltpu.SemaphoreType.DMA,
            pltpu.SemaphoreType.DMA((2, 2)),
            pltpu.SemaphoreType.DMA((2,)),
            pltpu.SemaphoreType.DMA,
        ],
        compiler_params=pltpu.CompilerParams(vmem_limit_bytes=48 << 20),
        name=name,
    )(place, *pieces, up, down)


def local(tokens, expert_ids, gate_weights, up_weights, down_weights):
    x, zl, zh = lax.axis_index("x"), lax.axis_index("zl"), lax.axis_index("zh")
    place = jnp.stack([zh * 4 + zl, x * 4 + zl]).astype(jnp.int32)
    picked = expert_ids[:, :, None] == jnp.arange(16, dtype=jnp.int32)
    dense = jnp.sum(jnp.where(picked, gate_weights[:, :, None], 0.0), axis=1)
    down = down_weights[0]

    b40 = jnp.concatenate([tokens[32:], weight_rows(dense[32:])])
    a40 = jnp.concatenate([tokens[:32], weight_rows(dense[:32])])
    bl, br = [tokens[32:]], [b40]
    for step in range(3):
        bl.append(permute_z(bl[-1], 1))
        br.append(permute_z(br[-1], -1))
        if step == 0:
            a1, a2, a3 = permute_x(a40, -1), permute_x(a40, 2), permute_x(a40, 1)
    b_far = permute_z(bl[3], 1)

    a_by_x = [a40, a1, a2, a3]
    a_tokens = jnp.concatenate([v[:32] for v in a_by_x])
    a0 = jnp.concatenate([a_tokens, pick_rows([v[32:] for v in a_by_x])])
    al, ar = [a_tokens], [a0]
    up = jnp.transpose(up_weights[0], (1, 0, 2))
    for step in range(3):
        al.append(permute_z(al[-1], 1))
        ar.append(permute_z(ar[-1], -1))
        if step == 1:
            al[2], ar[2], up = fence(al[2], ar[2], up)

    b_rows = pick_rows([v[32:] for v in br])
    b0 = jnp.concatenate([v[:32] for v in br] + [b_far, bl[3], bl[2], bl[1], b_rows])
    b_left = permute_x(b0, 1)
    b_right = permute_x(b0, -1)
    b_far0 = permute_x(jnp.concatenate([b_left[:128], b_left[256:]]), 1)
    b_far1 = permute_x(b_right[128:256], -1)

    def plan_b(sources):
        loads, stores = [], []
        for i, (near, far) in enumerate(sources):
            for q in range(4):
                loads.append((near[0], near[1] + q * 32, 32, i * 128 + q * 32, q))
                loads.append((far[0], far[1] + q * 32, 32, i * 128 + q * 32, q + 4))
                stores.append((i, 0, 32, i * 128 + q * 32, q))
        return loads, stores

    loads, stores = plan_b([((i, 0), (i, 128)) for i in range(3)])
    y_b0, y_b1, y_b3 = expert(
        place, [b0, b_right, b_left], up, down, loads, [(i, 256) for i in range(3)], stores, [256] * 3, "experts_b013"
    )
    al[3], ar[3], y_b0, y_b1, y_b3 = fence(al[3], ar[3], y_b0, y_b1, y_b3)
    a_far0 = permute_z(al[3][:64], 1)
    a_far1 = permute_z(ar[3][64:128], -1)
    loads, stores = plan_b([((0, 0), (1, 0))])
    (y_b2,) = expert(place, [b_far0, b_far1], up, down, loads, [(0, 128)], stores, [256], "experts_b2")

    a_far0, a_far1, y_b2 = fence(a_far0, a_far1, y_b2)
    pieces = [*ar, a_far0, a_far1, al[3], al[2], al[1]]
    loads = [(d, 0, 128, d * 128, d) for d in range(4)]
    loads += [(4, 0, 64, 0, 4), (5, 0, 64, 64, 4)]
    loads += [(d + 1, 0, 128, (d - 4) * 128, d) for d in range(5, 8)]
    stores = [(0, 0, 128, q * 128, q) for q in range(4)]
    (y_a,) = expert(place, pieces, up, down, loads, [(d, 128) for d in range(4)], stores, [1024], "experts_a")
    y_a = [y_a[d * 128 : (d + 1) * 128] for d in range(8)]

    bl = permute_x(halves(y_b2)[0], 1)
    br = permute_x(halves(y_b2)[1], -1)
    al = permute_z(halves(y_a[4])[0], 1)
    ar = permute_z(halves(y_a[4])[1], -1)
    al, ar, bl, br = fence(al, ar, bl, br)
    al = permute_z(add_half(al, y_a[3], 0), 1)
    ar = permute_z(add_half(ar, y_a[5], 1), -1)
    bl = permute_x(add_half(bl, y_b1, 0), 1)
    br = permute_x(add_half(br, y_b3, 1), -1)
    al, ar = fence(al, ar)
    al = permute_z(add(al, y_a[2]), 1)
    ar = permute_z(add(ar, y_a[6]), -1)
    al, ar, bl, br = fence(al, ar, bl, br)
    s_b = (y_b0.astype(F32) + bl.astype(F32) + br.astype(F32)).astype(BF)
    s_b = [s_b[d * 32 : (d + 1) * 32] for d in range(8)]
    al = permute_z(add(al, y_a[1]), 1)
    ar = permute_z(add(ar, y_a[7]), -1)
    bl = permute_z(s_b[4], 1)
    br = permute_z(s_b[5], -1)
    bl, br = fence(bl, br)
    bl = permute_z(add(bl, s_b[3]), 1)
    br = permute_z(add(br, s_b[6]), -1)
    al, ar, bl, br = fence(al, ar, bl, br)
    s_a = y_a[0].astype(F32) + al.astype(F32) + ar.astype(F32)
    bl = permute_z(add(bl, s_b[2]), 1)
    br = permute_z(add(br, s_b[7]), -1)
    bl = permute_z(add(bl, s_b[1]), 1)
    out_b = s_b[0].astype(F32) + bl.astype(F32) + br.astype(F32)
    far = [s_a[d * 32 : (d + 1) * 32].astype(BF) for d in range(1, 4)]
    got = [permute_x(far[0], 1), permute_x(far[1], 2), permute_x(far[2], 3)]
    out_a = s_a[:32] + got[0].astype(F32) + got[1].astype(F32) + got[2].astype(F32)
    return jnp.concatenate([out_a, out_b]).astype(BF)


def solution(mesh):
    fine = Mesh(mesh.devices.reshape(4, 4, 2, 4, 2), ("x", "zl", "zh", "y", "core"))
    rows = ("x", "zl", "y", "core")
    in_specs = (
        P(rows, "zh"),
        P(rows, None),
        P(rows, None),
        P(("x", "zl"), None, None, "zh"),
        P(("x", "zl"), "zh", None),
    )
    return jax.shard_map(
        local, mesh=fine, in_specs=in_specs, out_specs=P(rows, "zh"), check_vma=False
    )
```

```python
import functools

import jax
import jax.numpy as jnp
from jax import lax
from jax.experimental import pallas as pl
from jax.experimental.pallas import tpu as pltpu
from jax.sharding import Mesh
from jax.sharding import PartitionSpec as P

ZAX = ("zl", "zh")
BF = jnp.bfloat16
F32 = jnp.float32


def permute_x(v, step):
    return lax.ppermute(v, "x", [(i, (i + step) % 4) for i in range(4)])


def permute_z(v, step):
    index = lambda z: (z % 4) * 2 + z // 4
    return lax.ppermute(v, ZAX, [(index(z), index((z + step) % 8)) for z in range(8)])


def halves(v):
    n = v.shape[0] // 2
    return v[:n], v[n:]


def add(a, b):
    return (a.astype(F32) + b.astype(F32)).astype(BF)


def add_half(part, whole, which):
    w0, w1 = halves(whole)
    if which == 0:
        return jnp.concatenate([add(part, w0), w1])
    return jnp.concatenate([w0, add(part, w1)])


def fence(*values):
    return lax.optimization_barrier(values)


def weight_rows(dense):
    high = lax.reduce_precision(dense, 8, 7)
    rest = dense - high
    mid = lax.reduce_precision(rest, 8, 7)
    parts = jnp.stack([high, mid, rest - mid]).transpose(0, 2, 1).reshape(1, 1536)
    return jnp.broadcast_to(jnp.pad(parts.astype(BF), ((0, 0), (0, 512))), (8, 2048))


def pick_rows(blocks):
    row = lax.broadcasted_iota(jnp.int32, (8, 2048), 0)
    out = blocks[0]
    for r, block in enumerate(blocks[1:], 1):
        out = jnp.where(row == r, block, out)
    return out


def expert_kernel(loads, blocks, stores, n_in, n_out, place_ref, *refs):
    ins = refs[:n_in]
    up_ref, down_ref = refs[n_in : n_in + 2]
    outs = refs[n_in + 2 : n_in + 2 + n_out]
    x_buf, up_buf, down_buf, hidden, y_buf, rows_buf, w_buf, sem_x, sem_up, sem_down, sem_y = refs[n_in + 2 + n_out :]
    z, expert_num = place_ref[0], place_ref[1]

    def half_of(d):
        return lax.div(lax.rem(z + d, 8), 4)

    in_copies = [
        pltpu.make_async_copy(
            ins[ref].at[pl.ds(start, rows)],
            x_buf.at[pl.ds(row, rows), pl.ds(pl.multiple_of(half_of(d) * 2048, 2048), 2048)],
            sem_x,
        )
        for ref, start, rows, row, d in loads
    ] + [
        pltpu.make_async_copy(ins[ref].at[pl.ds(start, 8)], rows_buf.at[i], sem_x)
        for i, (ref, start) in enumerate(blocks)
    ]
    ups = [
        [
            pltpu.make_async_copy(
                up_ref.at[g, :, pl.ds(n * 256, 256)],
                up_buf.at[n, :, pl.ds(g * 256, 256)],
                sem_up.at[n, g],
            )
            for g in range(2)
        ]
        for n in range(2)
    ]
    downs = [
        pltpu.make_async_copy(
            down_ref.at[:, pl.ds(h * 2048, 2048)], down_buf.at[:, pl.ds(h * 2048, 2048)], sem_down.at[h]
        )
        for h in range(2)
    ]
    for c in [*in_copies, *ups[0], *ups[1], *downs]:
        c.start()
    for c in in_copies:
        c.wait()

    group = pl.multiple_of(lax.div(expert_num, 4) * 128, 128)
    lane = lax.broadcasted_iota(jnp.int32, (32, 128), 1)
    token = lax.broadcasted_iota(jnp.int32, (32, 128), 0)
    mine = lane == lax.rem(expert_num, 4) * 32 + token
    for i in range(len(blocks)):
        parts = [rows_buf[i, :, pl.ds(group + part * 512, 128)].astype(F32) for part in range(3)]
        total = parts[0] + parts[1] + parts[2]
        for j in range(4):
            picked = jnp.where(mine, jnp.broadcast_to(total[j : j + 1], (32, 128)), 0.0)
            w_buf[i * 128 + j * 32 : i * 128 + (j + 1) * 32, :] = jnp.broadcast_to(
                jnp.sum(picked, axis=1, keepdims=True), (32, 128)
            )

    for n in range(2):
        for c in ups[n]:
            c.wait()
        both = jnp.dot(x_buf[...], up_buf[n], preferred_element_type=F32)
        gate, up = both[:, :256], both[:, 256:]
        hidden[:, n * 256 : (n + 1) * 256] = (gate / (1.0 + jnp.exp(-gate)) * up).astype(BF)
    w = w_buf[:, :1]
    out_copies = []
    for h in range(2):
        downs[h].wait()
        for n in range(2):
            at = pl.ds(h * 2048 + n * 1024, 1024)
            y = jnp.dot(hidden[...], down_buf[:, at], preferred_element_type=F32)
            y_buf[:, at] = (y * w).astype(BF)
        for ref, start, rows, row, p in stores:
            d = p + 4 * lax.rem(half_of(p) + h, 2)
            c = pltpu.make_async_copy(
                y_buf.at[pl.ds(row, rows), pl.ds(h * 2048, 2048)],
                outs[ref].at[pl.ds(pl.multiple_of(start + d * rows, rows), rows)],
                sem_y,
            )
            c.start()
            out_copies.append(c)
    for c in out_copies:
        c.wait()


def expert(place, pieces, up, down, loads, blocks, stores, out_rows, name):
    n_in, n_out, rows = len(pieces), len(out_rows), len(blocks) * 128
    any_spec = pl.BlockSpec(memory_space=pl.ANY)
    return pl.pallas_call(
        functools.partial(expert_kernel, loads, blocks, stores, n_in, n_out),
        out_shape=[jax.ShapeDtypeStruct((r, 2048), BF) for r in out_rows],
        in_specs=[pl.BlockSpec(memory_space=pltpu.SMEM)] + [any_spec] * (n_in + 2),
        out_specs=[any_spec] * n_out,
        scratch_shapes=[
            pltpu.VMEM((rows, 4096), BF),
            pltpu.VMEM((2, 4096, 512), BF),
            pltpu.VMEM((512, 4096), BF),
            pltpu.VMEM((rows, 512), BF),
            pltpu.VMEM((rows, 4096), BF),
            pltpu.VMEM((len(blocks), 8, 2048), BF),
            pltpu.VMEM((rows, 128), F32),
            pltpu.SemaphoreType.DMA,
            pltpu.SemaphoreType.DMA((2, 2)),
            pltpu.SemaphoreType.DMA((2,)),
            pltpu.SemaphoreType.DMA,
        ],
        compiler_params=pltpu.CompilerParams(vmem_limit_bytes=48 << 20),
        name=name,
    )(place, *pieces, up, down)


def local(tokens, expert_ids, gate_weights, up_weights, down_weights):
    x, zl, zh = lax.axis_index("x"), lax.axis_index("zl"), lax.axis_index("zh")
    place = jnp.stack([zh * 4 + zl, x * 4 + zl]).astype(jnp.int32)
    picked = expert_ids[:, :, None] == jnp.arange(16, dtype=jnp.int32)
    dense = jnp.sum(jnp.where(picked, gate_weights[:, :, None], 0.0), axis=1)
    down = down_weights[0]

    b40 = jnp.concatenate([tokens[32:], weight_rows(dense[32:])])
    a40 = jnp.concatenate([tokens[:32], weight_rows(dense[:32])])
    b_by_z = [b40, permute_z(b40, -1), None, permute_z(b40, -3), None, permute_z(tokens[32:], 3), None, permute_z(tokens[32:], 1)]
    a1, a2, a3 = permute_x(a40, -1), permute_x(a40, 2), permute_x(a40, 1)
    b_by_z[2] = permute_z(b_by_z[1], -1)
    b_by_z[6], b_by_z[4] = halves(permute_z(jnp.concatenate([b_by_z[7], b_by_z[5]]), 1))

    a_by_x = [a40, a1, a2, a3]
    a_tokens = jnp.concatenate([v[:32] for v in a_by_x])
    a0 = jnp.concatenate([a_tokens, pick_rows([v[32:] for v in a_by_x])])
    al, ar = [a_tokens], [a0]
    up = jnp.transpose(up_weights[0], (1, 0, 2))
    al.append(permute_z(al[0], 1))
    ar.append(permute_z(ar[0], -1))
    b_rows = pick_rows([v[32:] for v in b_by_z[:4]])
    b0 = jnp.concatenate([v[:32] for v in b_by_z] + [b_rows])
    b_left = permute_x(b0, 1)
    b_right = permute_x(b0, -1)
    al[1], ar[1], up = fence(al[1], ar[1], up)
    al.append(permute_z(al[1], 1))
    ar.append(permute_z(ar[1], -1))

    def plan_b(sources):
        loads, stores = [], []
        for i, (near, far) in enumerate(sources):
            for q in range(4):
                loads.append((near[0], near[1] + q * 32, 32, i * 128 + q * 32, q))
                loads.append((far[0], far[1] + q * 32, 32, i * 128 + q * 32, q + 4))
                stores.append((i, 0, 32, i * 128 + q * 32, q))
        return loads, stores

    loads, stores = plan_b([((0, 0), (0, 128))])
    (y_b0,) = expert(place, [b0], up, down, loads, [(0, 256)], stores, [256], "experts_b0")
    al[2], ar[2], y_b0 = fence(al[2], ar[2], y_b0)
    al.append(permute_z(al[2], 1))
    ar.append(permute_z(ar[2], -1))
    b_far0 = permute_x(jnp.concatenate([b_left[:128], b_left[256:]]), 1)
    b_far1 = permute_x(b_right[128:256], -1)
    loads, stores = plan_b([((i, 0), (i, 128)) for i in range(2)])
    y_b1, y_b3 = expert(
        place, [b_right, b_left], up, down, loads, [(i, 256) for i in range(2)], stores, [256] * 2, "experts_b13"
    )
    al[3], ar[3], y_b1, y_b3 = fence(al[3], ar[3], y_b1, y_b3)
    a_far0 = permute_z(al[3][:64], 1)
    a_far1 = permute_z(ar[3][64:128], -1)
    loads, stores = plan_b([((0, 0), (1, 0))])
    (y_b2,) = expert(place, [b_far0, b_far1], up, down, loads, [(0, 128)], stores, [256], "experts_b2")

    a_far0, a_far1, y_b2 = fence(a_far0, a_far1, y_b2)
    pieces = [*ar, a_far0, a_far1, al[3], al[2], al[1]]
    loads = [(d, 0, 128, d * 128, d) for d in range(4)]
    loads += [(4, 0, 64, 0, 4), (5, 0, 64, 64, 4)]
    loads += [(d + 1, 0, 128, (d - 4) * 128, d) for d in range(5, 8)]
    stores = [(0, 0, 128, q * 128, q) for q in range(4)]
    (y_a,) = expert(place, pieces, up, down, loads, [(d, 128) for d in range(4)], stores, [1024], "experts_a")
    y_a = [y_a[d * 128 : (d + 1) * 128] for d in range(8)]

    bl = permute_x(halves(y_b2)[0], 1)
    br = permute_x(halves(y_b2)[1], -1)
    al = permute_z(halves(y_a[4])[0], 1)
    ar = permute_z(halves(y_a[4])[1], -1)
    al, ar, bl, br = fence(al, ar, bl, br)
    al = permute_z(add_half(al, y_a[3], 0), 1)
    ar = permute_z(add_half(ar, y_a[5], 1), -1)
    bl = permute_x(add_half(bl, y_b1, 0), 1)
    br = permute_x(add_half(br, y_b3, 1), -1)
    al = permute_z(add(al, y_a[2]), 1)
    ar = permute_z(add(ar, y_a[6]), -1)
    al, ar, bl, br = fence(al, ar, bl, br)
    al = permute_z(add(al, y_a[1]), 1)
    ar = permute_z(add(ar, y_a[7]), -1)
    s_b = (y_b0.astype(F32) + bl.astype(F32) + br.astype(F32)).astype(BF)
    s_b = [s_b[d * 32 : (d + 1) * 32] for d in range(8)]
    to7, to5 = halves(permute_z(jnp.concatenate([s_b[6], s_b[4]]), -1))
    to1 = permute_z(s_b[2], 1)
    got = [
        permute_z(s_b[3], 3),
        permute_z(add(to1, s_b[1]), 1),
        permute_z(add(to7, s_b[7]), -1),
        permute_z(add(to5, s_b[5]), -3),
    ]
    out_b = s_b[0].astype(F32) + sum(v.astype(F32) for v in got)
    s_a = y_a[0].astype(F32) + al.astype(F32) + ar.astype(F32)
    far = [s_a[d * 32 : (d + 1) * 32].astype(BF) for d in range(1, 4)]
    got = [permute_x(far[0], 1), permute_x(far[1], 2), permute_x(far[2], 3)]
    out_a = s_a[:32] + got[0].astype(F32) + got[1].astype(F32) + got[2].astype(F32)
    return jnp.concatenate([out_a, out_b]).astype(BF)


def solution(mesh):
    fine = Mesh(mesh.devices.reshape(4, 4, 2, 4, 2), ("x", "zl", "zh", "y", "core"))
    rows = ("x", "zl", "y", "core")
    in_specs = (
        P(rows, "zh"),
        P(rows, None),
        P(rows, None),
        P(("x", "zl"), None, None, "zh"),
        P(("x", "zl"), "zh", None),
    )
    return jax.shard_map(
        local, mesh=fine, in_specs=in_specs, out_specs=P(rows, "zh"), check_vma=False
    )
```

```python
import functools

import jax
import jax.numpy as jnp
from jax import lax
from jax.experimental import pallas as pl
from jax.experimental.pallas import tpu as pltpu
from jax.sharding import Mesh
from jax.sharding import PartitionSpec as P

ZAX = ("zl", "zh")
BF = jnp.bfloat16
F32 = jnp.float32


def permute_x(v, step):
    return lax.ppermute(v, "x", [(i, (i + step) % 4) for i in range(4)])


def permute_z(v, step):
    index = lambda z: (z % 4) * 2 + z // 4
    return lax.ppermute(v, ZAX, [(index(z), index((z + step) % 8)) for z in range(8)])


def halves(v):
    n = v.shape[0] // 2
    return v[:n], v[n:]


def add(a, b):
    return (a.astype(F32) + b.astype(F32)).astype(BF)


def add_half(part, whole, which):
    w0, w1 = halves(whole)
    if which == 0:
        return jnp.concatenate([add(part, w0), w1])
    return jnp.concatenate([w0, add(part, w1)])


def fence(*values):
    return lax.optimization_barrier(values)


def weight_rows(dense):
    high = lax.reduce_precision(dense, 8, 7)
    rest = dense - high
    mid = lax.reduce_precision(rest, 8, 7)
    parts = jnp.stack([high, mid, rest - mid]).transpose(0, 2, 1).reshape(1, 1536)
    return jnp.broadcast_to(jnp.pad(parts.astype(BF), ((0, 0), (0, 512))), (8, 2048))


def pick_rows(blocks):
    row = lax.broadcasted_iota(jnp.int32, (8, 2048), 0)
    out = blocks[0]
    for r, block in enumerate(blocks[1:], 1):
        out = jnp.where(row == r, block, out)
    return out


def expert_kernel(loads, blocks, stores, n_in, n_out, place_ref, *refs):
    ins = refs[:n_in]
    up_ref, down_ref = refs[n_in : n_in + 2]
    outs = refs[n_in + 2 : n_in + 2 + n_out]
    x_buf, up_buf, down_buf, hidden, y_buf, rows_buf, w_buf, sem_x, sem_up, sem_down, sem_y = refs[n_in + 2 + n_out :]
    z, expert_num = place_ref[0], place_ref[1]

    def half_of(d):
        return lax.div(lax.rem(z + d, 8), 4)

    in_copies = [
        pltpu.make_async_copy(
            ins[ref].at[pl.ds(start, rows)],
            x_buf.at[pl.ds(row, rows), pl.ds(pl.multiple_of(half_of(d) * 2048, 2048), 2048)],
            sem_x,
        )
        for ref, start, rows, row, d in loads
    ] + [
        pltpu.make_async_copy(ins[ref].at[pl.ds(start, 8)], rows_buf.at[i], sem_x)
        for i, (ref, start) in enumerate(blocks)
    ]
    ups = [
        [
            pltpu.make_async_copy(
                up_ref.at[g, :, pl.ds(n * 256, 256)],
                up_buf.at[n, :, pl.ds(g * 256, 256)],
                sem_up.at[n, g],
            )
            for g in range(2)
        ]
        for n in range(2)
    ]
    downs = [
        pltpu.make_async_copy(
            down_ref.at[:, pl.ds(h * 2048, 2048)], down_buf.at[:, pl.ds(h * 2048, 2048)], sem_down.at[h]
        )
        for h in range(2)
    ]
    for c in [*in_copies, *ups[0], *ups[1], *downs]:
        c.start()
    for c in in_copies:
        c.wait()

    group = pl.multiple_of(lax.div(expert_num, 4) * 128, 128)
    lane = lax.broadcasted_iota(jnp.int32, (32, 128), 1)
    token = lax.broadcasted_iota(jnp.int32, (32, 128), 0)
    mine = lane == lax.rem(expert_num, 4) * 32 + token
    for i in range(len(blocks)):
        parts = [rows_buf[i, :, pl.ds(group + part * 512, 128)].astype(F32) for part in range(3)]
        total = parts[0] + parts[1] + parts[2]
        for j in range(4):
            picked = jnp.where(mine, jnp.broadcast_to(total[j : j + 1], (32, 128)), 0.0)
            w_buf[i * 128 + j * 32 : i * 128 + (j + 1) * 32, :] = jnp.broadcast_to(
                jnp.sum(picked, axis=1, keepdims=True), (32, 128)
            )

    for n in range(2):
        for c in ups[n]:
            c.wait()
        both = jnp.dot(x_buf[...], up_buf[n], preferred_element_type=F32)
        gate, up = both[:, :256], both[:, 256:]
        hidden[:, n * 256 : (n + 1) * 256] = (gate / (1.0 + jnp.exp(-gate)) * up).astype(BF)
    w = w_buf[:, :1]
    out_copies = []
    for h in range(2):
        downs[h].wait()
        for n in range(2):
            at = pl.ds(h * 2048 + n * 1024, 1024)
            y = jnp.dot(hidden[...], down_buf[:, at], preferred_element_type=F32)
            y_buf[:, at] = (y * w).astype(BF)
        for ref, start, rows, row, p in stores:
            d = p + 4 * lax.rem(half_of(p) + h, 2)
            c = pltpu.make_async_copy(
                y_buf.at[pl.ds(row, rows), pl.ds(h * 2048, 2048)],
                outs[ref].at[pl.ds(pl.multiple_of(start + d * rows, rows), rows)],
                sem_y,
            )
            c.start()
            out_copies.append(c)
    for c in out_copies:
        c.wait()


def expert(place, pieces, up, down, loads, blocks, stores, out_rows, name):
    n_in, n_out, rows = len(pieces), len(out_rows), len(blocks) * 128
    any_spec = pl.BlockSpec(memory_space=pl.ANY)
    return pl.pallas_call(
        functools.partial(expert_kernel, loads, blocks, stores, n_in, n_out),
        out_shape=[jax.ShapeDtypeStruct((r, 2048), BF) for r in out_rows],
        in_specs=[pl.BlockSpec(memory_space=pltpu.SMEM)] + [any_spec] * (n_in + 2),
        out_specs=[any_spec] * n_out,
        scratch_shapes=[
            pltpu.VMEM((rows, 4096), BF),
            pltpu.VMEM((2, 4096, 512), BF),
            pltpu.VMEM((512, 4096), BF),
            pltpu.VMEM((rows, 512), BF),
            pltpu.VMEM((rows, 4096), BF),
            pltpu.VMEM((len(blocks), 8, 2048), BF),
            pltpu.VMEM((rows, 128), F32),
            pltpu.SemaphoreType.DMA,
            pltpu.SemaphoreType.DMA((2, 2)),
            pltpu.SemaphoreType.DMA((2,)),
            pltpu.SemaphoreType.DMA,
        ],
        compiler_params=pltpu.CompilerParams(vmem_limit_bytes=48 << 20),
        name=name,
    )(place, *pieces, up, down)


def local(tokens, expert_ids, gate_weights, up_weights, down_weights):
    x, zl, zh = lax.axis_index("x"), lax.axis_index("zl"), lax.axis_index("zh")
    place = jnp.stack([zh * 4 + zl, x * 4 + zl]).astype(jnp.int32)
    picked = expert_ids[:, :, None] == jnp.arange(16, dtype=jnp.int32)
    dense = jnp.sum(jnp.where(picked, gate_weights[:, :, None], 0.0), axis=1)
    down = down_weights[0]

    b40 = jnp.concatenate([tokens[32:], weight_rows(dense[32:])])
    a40 = jnp.concatenate([tokens[:32], weight_rows(dense[:32])])
    b_by_z = [b40, permute_z(b40, -1), None, permute_z(b40, -3), None, permute_z(tokens[32:], 3), None, permute_z(tokens[32:], 1)]
    a1, a2, a3 = permute_x(a40, -1), permute_x(a40, 2), permute_x(a40, 1)
    a_by_x = [a40, a1, a2, a3]
    a_tokens = jnp.concatenate([v[:32] for v in a_by_x])
    a0 = jnp.concatenate([a_tokens, pick_rows([v[32:] for v in a_by_x])])
    al = [a_tokens, permute_z(a_tokens, 1)]
    ar = [a0, permute_z(a0, -1)]
    up = jnp.transpose(up_weights[0], (1, 0, 2))
    al[1], ar[1], up, *near = fence(al[1], ar[1], up, b_by_z[1], b_by_z[7], b_by_z[5])
    b_by_z[1], b_by_z[7], b_by_z[5] = near
    b_by_z[2] = permute_z(b_by_z[1], -1)
    b_by_z[6], b_by_z[4] = halves(permute_z(jnp.concatenate([b_by_z[7], b_by_z[5]]), 1))
    b_rows = pick_rows([v[32:] for v in b_by_z[:4]])
    b0 = jnp.concatenate([v[:32] for v in b_by_z] + [b_rows])
    b_left = permute_x(b0, 1)
    b_right = permute_x(b0, -1)
    al.append(permute_z(al[1], 1))
    ar.append(permute_z(ar[1], -1))

    def plan_b(sources):
        loads, stores = [], []
        for i, (near, far) in enumerate(sources):
            for q in range(4):
                loads.append((near[0], near[1] + q * 32, 32, i * 128 + q * 32, q))
                loads.append((far[0], far[1] + q * 32, 32, i * 128 + q * 32, q + 4))
                stores.append((i, 0, 32, i * 128 + q * 32, q))
        return loads, stores

    loads, stores = plan_b([((0, 0), (0, 128))])
    (y_b0,) = expert(place, [b0], up, down, loads, [(0, 256)], stores, [256], "experts_b0")
    al[2], ar[2], y_b0 = fence(al[2], ar[2], y_b0)
    al.append(permute_z(al[2], 1))
    ar.append(permute_z(ar[2], -1))
    b_far0 = permute_x(jnp.concatenate([b_left[:128], b_left[256:]]), 1)
    b_far1 = permute_x(b_right[128:256], -1)
    loads, stores = plan_b([((i, 0), (i, 128)) for i in range(2)])
    y_b1, y_b3 = expert(
        place, [b_right, b_left], up, down, loads, [(i, 256) for i in range(2)], stores, [256] * 2, "experts_b13"
    )
    al[3], ar[3], y_b1, y_b3 = fence(al[3], ar[3], y_b1, y_b3)
    a_far0 = permute_z(al[3][:64], 1)
    a_far1 = permute_z(ar[3][64:128], -1)
    loads, stores = plan_b([((0, 0), (1, 0))])
    (y_b2,) = expert(place, [b_far0, b_far1], up, down, loads, [(0, 128)], stores, [256], "experts_b2")

    a_far0, a_far1, y_b2 = fence(a_far0, a_far1, y_b2)
    pieces = [*ar, a_far0, a_far1, al[3], al[2], al[1]]
    loads = [(d, 0, 128, d * 128, d) for d in range(4)]
    loads += [(4, 0, 64, 0, 4), (5, 0, 64, 64, 4)]
    loads += [(d + 1, 0, 128, (d - 4) * 128, d) for d in range(5, 8)]
    stores = [(0, 0, 128, q * 128, q) for q in range(4)]
    (y_a,) = expert(place, pieces, up, down, loads, [(d, 128) for d in range(4)], stores, [1024], "experts_a")
    y_a = [y_a[d * 128 : (d + 1) * 128] for d in range(8)]

    bl = permute_x(halves(y_b2)[0], 1)
    br = permute_x(halves(y_b2)[1], -1)
    al = permute_z(halves(y_a[4])[0], 1)
    ar = permute_z(halves(y_a[4])[1], -1)
    al, ar, bl, br = fence(al, ar, bl, br)
    al = permute_z(add_half(al, y_a[3], 0), 1)
    ar = permute_z(add_half(ar, y_a[5], 1), -1)
    bl = permute_x(add_half(bl, y_b1, 0), 1)
    br = permute_x(add_half(br, y_b3, 1), -1)
    al, ar = fence(al, ar)
    al = permute_z(add(al, y_a[2]), 1)
    ar = permute_z(add(ar, y_a[6]), -1)
    al, ar, bl, br = fence(al, ar, bl, br)
    s_b = (y_b0.astype(F32) + bl.astype(F32) + br.astype(F32)).astype(BF)
    s_b = [s_b[d * 32 : (d + 1) * 32] for d in range(8)]
    al = permute_z(add(al, y_a[1]), 1)
    ar = permute_z(add(ar, y_a[7]), -1)
    bl = permute_z(s_b[4], 1)
    br = permute_z(s_b[5], -1)
    bl, br = fence(bl, br)
    bl = permute_z(add(bl, s_b[3]), 1)
    br = permute_z(add(br, s_b[6]), -1)
    al, ar, bl, br = fence(al, ar, bl, br)
    s_a = y_a[0].astype(F32) + al.astype(F32) + ar.astype(F32)
    bl = permute_z(add(bl, s_b[2]), 1)
    br = permute_z(add(br, s_b[7]), -1)
    bl = permute_z(add(bl, s_b[1]), 1)
    out_b = s_b[0].astype(F32) + bl.astype(F32) + br.astype(F32)
    far = [s_a[d * 32 : (d + 1) * 32].astype(BF) for d in range(1, 4)]
    got = [permute_x(far[0], 1), permute_x(far[1], 2), permute_x(far[2], 3)]
    out_a = s_a[:32] + got[0].astype(F32) + got[1].astype(F32) + got[2].astype(F32)
    return jnp.concatenate([out_a, out_b]).astype(BF)


def solution(mesh):
    fine = Mesh(mesh.devices.reshape(4, 4, 2, 4, 2), ("x", "zl", "zh", "y", "core"))
    rows = ("x", "zl", "y", "core")
    in_specs = (
        P(rows, "zh"),
        P(rows, None),
        P(rows, None),
        P(("x", "zl"), None, None, "zh"),
        P(("x", "zl"), "zh", None),
    )
    return jax.shard_map(
        local, mesh=fine, in_specs=in_specs, out_specs=P(rows, "zh"), check_vma=False
    )
```

```python
import functools

import jax
import jax.numpy as jnp
from jax import lax
from jax.experimental import pallas as pl
from jax.experimental.pallas import tpu as pltpu
from jax.sharding import Mesh
from jax.sharding import PartitionSpec as P

ZAX = ("zl", "zh")
BF = jnp.bfloat16
F32 = jnp.float32


def permute_x(v, step):
    return lax.ppermute(v, "x", [(i, (i + step) % 4) for i in range(4)])


def permute_z(v, step):
    index = lambda z: (z % 4) * 2 + z // 4
    return lax.ppermute(v, ZAX, [(index(z), index((z + step) % 8)) for z in range(8)])


def halves(v):
    n = v.shape[0] // 2
    return v[:n], v[n:]


def add(a, b):
    return (a.astype(F32) + b.astype(F32)).astype(BF)


def add_half(part, whole, which):
    w0, w1 = halves(whole)
    if which == 0:
        return jnp.concatenate([add(part, w0), w1])
    return jnp.concatenate([w0, add(part, w1)])


def fence(*values):
    return lax.optimization_barrier(values)


def weight_rows(dense):
    high = lax.reduce_precision(dense, 8, 7)
    rest = dense - high
    mid = lax.reduce_precision(rest, 8, 7)
    parts = jnp.stack([high, mid, rest - mid]).transpose(0, 2, 1).reshape(1, 1536)
    return jnp.broadcast_to(jnp.pad(parts.astype(BF), ((0, 0), (0, 512))), (8, 2048))


def pick_rows(blocks):
    row = lax.broadcasted_iota(jnp.int32, (8, 2048), 0)
    out = blocks[0]
    for r, block in enumerate(blocks[1:], 1):
        out = jnp.where(row == r, block, out)
    return out


def expert_kernel(loads, blocks, stores, n_in, n_out, place_ref, *refs):
    ins = refs[:n_in]
    up_ref, down_ref = refs[n_in : n_in + 2]
    outs = refs[n_in + 2 : n_in + 2 + n_out]
    x_buf, up_buf, down_buf, hidden, y_buf, rows_buf, w_buf, sem_x, sem_up, sem_down, sem_y = refs[n_in + 2 + n_out :]
    z, expert_num = place_ref[0], place_ref[1]

    def half_of(d):
        return lax.div(lax.rem(z + d, 8), 4)

    in_copies = [
        pltpu.make_async_copy(
            ins[ref].at[pl.ds(start, rows)],
            x_buf.at[pl.ds(row, rows), pl.ds(pl.multiple_of(half_of(d) * 2048, 2048), 2048)],
            sem_x,
        )
        for ref, start, rows, row, d in loads
    ] + [
        pltpu.make_async_copy(ins[ref].at[pl.ds(start, 8)], rows_buf.at[i], sem_x)
        for i, (ref, start) in enumerate(blocks)
    ]
    ups = [
        [
            pltpu.make_async_copy(
                up_ref.at[g, :, pl.ds(n * 256, 256)],
                up_buf.at[n, :, pl.ds(g * 256, 256)],
                sem_up.at[n, g],
            )
            for g in range(2)
        ]
        for n in range(2)
    ]
    downs = [
        pltpu.make_async_copy(
            down_ref.at[:, pl.ds(h * 2048, 2048)], down_buf.at[:, pl.ds(h * 2048, 2048)], sem_down.at[h]
        )
        for h in range(2)
    ]
    for c in [*in_copies, *ups[0], *ups[1], *downs]:
        c.start()
    for c in in_copies:
        c.wait()

    group = pl.multiple_of(lax.div(expert_num, 4) * 128, 128)
    lane = lax.broadcasted_iota(jnp.int32, (32, 128), 1)
    token = lax.broadcasted_iota(jnp.int32, (32, 128), 0)
    mine = lane == lax.rem(expert_num, 4) * 32 + token
    for i in range(len(blocks)):
        parts = [rows_buf[i, :, pl.ds(group + part * 512, 128)].astype(F32) for part in range(3)]
        total = parts[0] + parts[1] + parts[2]
        for j in range(4):
            picked = jnp.where(mine, jnp.broadcast_to(total[j : j + 1], (32, 128)), 0.0)
            w_buf[i * 128 + j * 32 : i * 128 + (j + 1) * 32, :] = jnp.broadcast_to(
                jnp.sum(picked, axis=1, keepdims=True), (32, 128)
            )

    for n in range(2):
        for c in ups[n]:
            c.wait()
        both = jnp.dot(x_buf[...], up_buf[n], preferred_element_type=F32)
        gate, up = both[:, :256], both[:, 256:]
        hidden[:, n * 256 : (n + 1) * 256] = (gate / (1.0 + jnp.exp(-gate)) * up).astype(BF)
    w = w_buf[:, :1]
    out_copies = []
    for h in range(2):
        downs[h].wait()
        for n in range(2):
            at = pl.ds(h * 2048 + n * 1024, 1024)
            y = jnp.dot(hidden[...], down_buf[:, at], preferred_element_type=F32)
            y_buf[:, at] = (y * w).astype(BF)
        for ref, start, rows, row, p in stores:
            d = p + 4 * lax.rem(half_of(p) + h, 2)
            c = pltpu.make_async_copy(
                y_buf.at[pl.ds(row, rows), pl.ds(h * 2048, 2048)],
                outs[ref].at[pl.ds(pl.multiple_of(start + d * rows, rows), rows)],
                sem_y,
            )
            c.start()
            out_copies.append(c)
    for c in out_copies:
        c.wait()


def expert(place, pieces, up, down, loads, blocks, stores, out_rows, name):
    n_in, n_out, rows = len(pieces), len(out_rows), len(blocks) * 128
    any_spec = pl.BlockSpec(memory_space=pl.ANY)
    return pl.pallas_call(
        functools.partial(expert_kernel, loads, blocks, stores, n_in, n_out),
        out_shape=[jax.ShapeDtypeStruct((r, 2048), BF) for r in out_rows],
        in_specs=[pl.BlockSpec(memory_space=pltpu.SMEM)] + [any_spec] * (n_in + 2),
        out_specs=[any_spec] * n_out,
        scratch_shapes=[
            pltpu.VMEM((rows, 4096), BF),
            pltpu.VMEM((2, 4096, 512), BF),
            pltpu.VMEM((512, 4096), BF),
            pltpu.VMEM((rows, 512), BF),
            pltpu.VMEM((rows, 4096), BF),
            pltpu.VMEM((len(blocks), 8, 2048), BF),
            pltpu.VMEM((rows, 128), F32),
            pltpu.SemaphoreType.DMA,
            pltpu.SemaphoreType.DMA((2, 2)),
            pltpu.SemaphoreType.DMA((2,)),
            pltpu.SemaphoreType.DMA,
        ],
        compiler_params=pltpu.CompilerParams(vmem_limit_bytes=48 << 20),
        name=name,
    )(place, *pieces, up, down)


def local(tokens, expert_ids, gate_weights, up_weights, down_weights):
    x, zl, zh = lax.axis_index("x"), lax.axis_index("zl"), lax.axis_index("zh")
    place = jnp.stack([zh * 4 + zl, x * 4 + zl]).astype(jnp.int32)
    picked = expert_ids[:, :, None] == jnp.arange(16, dtype=jnp.int32)
    dense = jnp.sum(jnp.where(picked, gate_weights[:, :, None], 0.0), axis=1)
    down = down_weights[0]

    b40 = jnp.concatenate([tokens[32:], weight_rows(dense[32:])])
    a40 = jnp.concatenate([tokens[:32], weight_rows(dense[:32])])
    b_by_z = [b40, permute_z(b40, -1), None, permute_z(b40, -3), None, permute_z(tokens[32:], 3), None, permute_z(tokens[32:], 1)]
    a1, a2, a3 = permute_x(a40, -1), permute_x(a40, 2), permute_x(a40, 1)
    b_by_z[2] = permute_z(b_by_z[1], -1)
    b_by_z[6], b_by_z[4] = halves(permute_z(jnp.concatenate([b_by_z[7], b_by_z[5]]), 1))

    a_by_x = [a40, a1, a2, a3]
    a_tokens = jnp.concatenate([v[:32] for v in a_by_x])
    a0 = jnp.concatenate([a_tokens, pick_rows([v[32:] for v in a_by_x])])
    al, ar = [a_tokens], [a0]
    up = jnp.transpose(up_weights[0], (1, 0, 2))
    al.append(permute_z(al[0], 1))
    ar.append(permute_z(ar[0], -1))
    b_rows = pick_rows([v[32:] for v in b_by_z[:4]])
    b0 = jnp.concatenate([v[:32] for v in b_by_z] + [b_rows])
    b_left = permute_x(b0, 1)
    b_right = permute_x(b0, -1)
    al[1], ar[1], up = fence(al[1], ar[1], up)
    al.append(permute_z(al[1], 1))
    ar.append(permute_z(ar[1], -1))

    def plan_b(sources):
        loads, stores = [], []
        for i, (near, far) in enumerate(sources):
            for q in range(4):
                loads.append((near[0], near[1] + q * 32, 32, i * 128 + q * 32, q))
                loads.append((far[0], far[1] + q * 32, 32, i * 128 + q * 32, q + 4))
                stores.append((i, 0, 32, i * 128 + q * 32, q))
        return loads, stores

    loads, stores = plan_b([((0, 0), (0, 128))])
    (y_b0,) = expert(place, [b0], up, down, loads, [(0, 256)], stores, [256], "experts_b0")
    al[2], ar[2], y_b0 = fence(al[2], ar[2], y_b0)
    al.append(permute_z(al[2], 1))
    ar.append(permute_z(ar[2], -1))
    b_far0 = permute_x(jnp.concatenate([b_left[:128], b_left[256:]]), 1)
    b_far1 = permute_x(b_right[128:256], -1)
    loads, stores = plan_b([((i, 0), (i, 128)) for i in range(2)])
    y_b1, y_b3 = expert(
        place, [b_right, b_left], up, down, loads, [(i, 256) for i in range(2)], stores, [256] * 2, "experts_b13"
    )
    al[3], ar[3], y_b1, y_b3 = fence(al[3], ar[3], y_b1, y_b3)
    a_far0 = permute_z(al[3][:64], 1)
    a_far1 = permute_z(ar[3][64:128], -1)
    loads, stores = plan_b([((0, 0), (1, 0))])
    (y_b2,) = expert(place, [b_far0, b_far1], up, down, loads, [(0, 128)], stores, [256], "experts_b2")

    a_far0, a_far1, y_b2 = fence(a_far0, a_far1, y_b2)
    pieces = [*ar, a_far0, a_far1, al[3], al[2], al[1]]
    loads = [(d, 0, 128, d * 128, d) for d in range(4)]
    loads += [(4, 0, 64, 0, 4), (5, 0, 64, 64, 4)]
    loads += [(d + 1, 0, 128, (d - 4) * 128, d) for d in range(5, 8)]
    stores = [(0, 0, 128, q * 128, q) for q in range(4)]
    (y_a,) = expert(place, pieces, up, down, loads, [(d, 128) for d in range(4)], stores, [1024], "experts_a")
    y_a = [y_a[d * 128 : (d + 1) * 128] for d in range(8)]

    bl = permute_x(halves(y_b2)[0], 1)
    br = permute_x(halves(y_b2)[1], -1)
    al = permute_z(halves(y_a[4])[0], 1)
    ar = permute_z(halves(y_a[4])[1], -1)
    al, ar, bl, br = fence(al, ar, bl, br)
    al = permute_z(add_half(al, y_a[3], 0), 1)
    ar = permute_z(add_half(ar, y_a[5], 1), -1)
    bl = permute_x(add_half(bl, y_b1, 0), 1)
    br = permute_x(add_half(br, y_b3, 1), -1)
    al, ar = fence(al, ar)
    al = permute_z(add(al, y_a[2]), 1)
    ar = permute_z(add(ar, y_a[6]), -1)
    al, ar, bl, br = fence(al, ar, bl, br)
    s_b = (y_b0.astype(F32) + bl.astype(F32) + br.astype(F32)).astype(BF)
    s_b = [s_b[d * 32 : (d + 1) * 32] for d in range(8)]
    al = permute_z(add(al, y_a[1]), 1)
    ar = permute_z(add(ar, y_a[7]), -1)
    bl = permute_z(s_b[4], 1)
    br = permute_z(s_b[5], -1)
    bl, br = fence(bl, br)
    bl = permute_z(add(bl, s_b[3]), 1)
    br = permute_z(add(br, s_b[6]), -1)
    al, ar, bl, br = fence(al, ar, bl, br)
    s_a = y_a[0].astype(F32) + al.astype(F32) + ar.astype(F32)
    bl = permute_z(add(bl, s_b[2]), 1)
    br = permute_z(add(br, s_b[7]), -1)
    bl = permute_z(add(bl, s_b[1]), 1)
    out_b = s_b[0].astype(F32) + bl.astype(F32) + br.astype(F32)
    far = [s_a[d * 32 : (d + 1) * 32].astype(BF) for d in range(1, 4)]
    got = [permute_x(far[0], 1), permute_x(far[1], 2), permute_x(far[2], 3)]
    out_a = s_a[:32] + got[0].astype(F32) + got[1].astype(F32) + got[2].astype(F32)
    return jnp.concatenate([out_a, out_b]).astype(BF)


def solution(mesh):
    fine = Mesh(mesh.devices.reshape(4, 4, 2, 4, 2), ("x", "zl", "zh", "y", "core"))
    rows = ("x", "zl", "y", "core")
    in_specs = (
        P(rows, "zh"),
        P(rows, None),
        P(rows, None),
        P(("x", "zl"), None, None, "zh"),
        P(("x", "zl"), "zh", None),
    )
    return jax.shard_map(
        local, mesh=fine, in_specs=in_specs, out_specs=P(rows, "zh"), check_vma=False
    )
```

```python
import functools

import jax
import jax.numpy as jnp
from jax import lax
from jax.experimental import pallas as pl
from jax.experimental.pallas import tpu as pltpu
from jax.sharding import Mesh
from jax.sharding import PartitionSpec as P

ZAX = ("zl", "zh")
BF = jnp.bfloat16
F32 = jnp.float32


def permute_x(v, step):
    return lax.ppermute(v, "x", [(i, (i + step) % 4) for i in range(4)])


def permute_z(v, step):
    index = lambda z: (z % 4) * 2 + z // 4
    return lax.ppermute(v, ZAX, [(index(z), index((z + step) % 8)) for z in range(8)])


def halves(v):
    n = v.shape[0] // 2
    return v[:n], v[n:]


def add(a, b):
    return (a.astype(F32) + b.astype(F32)).astype(BF)


def add_half(part, whole, which):
    w0, w1 = halves(whole)
    if which == 0:
        return jnp.concatenate([add(part, w0), w1])
    return jnp.concatenate([w0, add(part, w1)])


def fence(*values):
    return lax.optimization_barrier(values)


def weight_rows(dense):
    high = lax.reduce_precision(dense, 8, 7)
    rest = dense - high
    mid = lax.reduce_precision(rest, 8, 7)
    parts = jnp.stack([high, mid, rest - mid]).transpose(0, 2, 1).reshape(1, 1536)
    return jnp.broadcast_to(jnp.pad(parts.astype(BF), ((0, 0), (0, 512))), (8, 2048))


def pick_rows(blocks):
    row = lax.broadcasted_iota(jnp.int32, (8, 2048), 0)
    out = blocks[0]
    for r, block in enumerate(blocks[1:], 1):
        out = jnp.where(row == r, block, out)
    return out


def expert_kernel(loads, blocks, stores, n_in, n_out, place_ref, *refs):
    ins = refs[:n_in]
    up_ref, down_ref = refs[n_in : n_in + 2]
    outs = refs[n_in + 2 : n_in + 2 + n_out]
    x_buf, up_buf, down_buf, hidden, y_buf, rows_buf, w_buf, sem_x, sem_up, sem_down, sem_y = refs[n_in + 2 + n_out :]
    z, expert_num = place_ref[0], place_ref[1]

    def half_of(d):
        return lax.div(lax.rem(z + d, 8), 4)

    in_copies = [
        pltpu.make_async_copy(
            ins[ref].at[pl.ds(start, rows)],
            x_buf.at[pl.ds(row, rows), pl.ds(pl.multiple_of(half_of(d) * 2048, 2048), 2048)],
            sem_x,
        )
        for ref, start, rows, row, d in loads
    ] + [
        pltpu.make_async_copy(ins[ref].at[pl.ds(start, 8)], rows_buf.at[i], sem_x)
        for i, (ref, start) in enumerate(blocks)
    ]
    ups = [
        [
            pltpu.make_async_copy(
                up_ref.at[g, :, pl.ds(n * 256, 256)],
                up_buf.at[n, :, pl.ds(g * 256, 256)],
                sem_up.at[n, g],
            )
            for g in range(2)
        ]
        for n in range(2)
    ]
    downs = [
        pltpu.make_async_copy(
            down_ref.at[:, pl.ds(h * 2048, 2048)], down_buf.at[:, pl.ds(h * 2048, 2048)], sem_down.at[h]
        )
        for h in range(2)
    ]
    for c in [*in_copies, *ups[0], *ups[1], *downs]:
        c.start()
    for c in in_copies:
        c.wait()

    group = pl.multiple_of(lax.div(expert_num, 4) * 128, 128)
    lane = lax.broadcasted_iota(jnp.int32, (32, 128), 1)
    token = lax.broadcasted_iota(jnp.int32, (32, 128), 0)
    mine = lane == lax.rem(expert_num, 4) * 32 + token
    for i in range(len(blocks)):
        parts = [rows_buf[i, :, pl.ds(group + part * 512, 128)].astype(F32) for part in range(3)]
        total = parts[0] + parts[1] + parts[2]
        for j in range(4):
            picked = jnp.where(mine, jnp.broadcast_to(total[j : j + 1], (32, 128)), 0.0)
            w_buf[i * 128 + j * 32 : i * 128 + (j + 1) * 32, :] = jnp.broadcast_to(
                jnp.sum(picked, axis=1, keepdims=True), (32, 128)
            )

    for n in range(2):
        for c in ups[n]:
            c.wait()
        both = jnp.dot(x_buf[...], up_buf[n], preferred_element_type=F32)
        gate, up = both[:, :256], both[:, 256:]
        hidden[:, n * 256 : (n + 1) * 256] = (gate / (1.0 + jnp.exp(-gate)) * up).astype(BF)
    w = w_buf[:, :1]
    out_copies = []
    for h in range(2):
        downs[h].wait()
        for n in range(2):
            at = pl.ds(h * 2048 + n * 1024, 1024)
            y = jnp.dot(hidden[...], down_buf[:, at], preferred_element_type=F32)
            y_buf[:, at] = (y * w).astype(BF)
        for ref, start, rows, row, p in stores:
            d = p + 4 * lax.rem(half_of(p) + h, 2)
            c = pltpu.make_async_copy(
                y_buf.at[pl.ds(row, rows), pl.ds(h * 2048, 2048)],
                outs[ref].at[pl.ds(pl.multiple_of(start + d * rows, rows), rows)],
                sem_y,
            )
            c.start()
            out_copies.append(c)
    for c in out_copies:
        c.wait()


def expert(place, pieces, up, down, loads, blocks, stores, out_rows, name):
    n_in, n_out, rows = len(pieces), len(out_rows), len(blocks) * 128
    any_spec = pl.BlockSpec(memory_space=pl.ANY)
    return pl.pallas_call(
        functools.partial(expert_kernel, loads, blocks, stores, n_in, n_out),
        out_shape=[jax.ShapeDtypeStruct((r, 2048), BF) for r in out_rows],
        in_specs=[pl.BlockSpec(memory_space=pltpu.SMEM)] + [any_spec] * (n_in + 2),
        out_specs=[any_spec] * n_out,
        scratch_shapes=[
            pltpu.VMEM((rows, 4096), BF),
            pltpu.VMEM((2, 4096, 512), BF),
            pltpu.VMEM((512, 4096), BF),
            pltpu.VMEM((rows, 512), BF),
            pltpu.VMEM((rows, 4096), BF),
            pltpu.VMEM((len(blocks), 8, 2048), BF),
            pltpu.VMEM((rows, 128), F32),
            pltpu.SemaphoreType.DMA,
            pltpu.SemaphoreType.DMA((2, 2)),
            pltpu.SemaphoreType.DMA((2,)),
            pltpu.SemaphoreType.DMA,
        ],
        compiler_params=pltpu.CompilerParams(vmem_limit_bytes=48 << 20),
        name=name,
    )(place, *pieces, up, down)


def local(tokens, expert_ids, gate_weights, up_weights, down_weights):
    x, zl, zh = lax.axis_index("x"), lax.axis_index("zl"), lax.axis_index("zh")
    place = jnp.stack([zh * 4 + zl, x * 4 + zl]).astype(jnp.int32)
    picked = expert_ids[:, :, None] == jnp.arange(16, dtype=jnp.int32)
    dense = jnp.sum(jnp.where(picked, gate_weights[:, :, None], 0.0), axis=1)
    down = down_weights[0]

    b40 = jnp.concatenate([tokens[32:], weight_rows(dense[32:])])
    a40 = jnp.concatenate([tokens[:32], weight_rows(dense[:32])])
    bl, br = [tokens[32:]], [b40]
    for step in range(3):
        bl.append(permute_z(bl[-1], 1))
        br.append(permute_z(br[-1], -1))
        if step == 0:
            a1, a2, a3 = permute_x(a40, -1), permute_x(a40, 2), permute_x(a40, 1)
    b_far = permute_z(bl[3], 1)

    a_by_x = [a40, a1, a2, a3]
    a_tokens = jnp.concatenate([v[:32] for v in a_by_x])
    a0 = jnp.concatenate([a_tokens, pick_rows([v[32:] for v in a_by_x])])
    al, ar = [a_tokens], [a0]
    up = jnp.transpose(up_weights[0], (1, 0, 2))
    for step in range(3):
        al.append(permute_z(al[-1], 1))
        ar.append(permute_z(ar[-1], -1))
        if step == 1:
            al[2], ar[2], up = fence(al[2], ar[2], up)

    b_rows = pick_rows([v[32:] for v in br])
    b0 = jnp.concatenate([v[:32] for v in br] + [b_far, bl[3], bl[2], bl[1], b_rows])
    b_left = permute_x(b0, 1)
    b_right = permute_x(b0, -1)
    b_far0 = permute_x(jnp.concatenate([b_left[:128], b_left[256:]]), 1)
    b_far1 = permute_x(b_right[128:256], -1)

    def plan_b(sources):
        loads, stores = [], []
        for i, (near, far) in enumerate(sources):
            for q in range(4):
                loads.append((near[0], near[1] + q * 32, 32, i * 128 + q * 32, q))
                loads.append((far[0], far[1] + q * 32, 32, i * 128 + q * 32, q + 4))
                stores.append((i, 0, 32, i * 128 + q * 32, q))
        return loads, stores

    loads, stores = plan_b([((i, 0), (i, 128)) for i in range(3)])
    y_b0, y_b1, y_b3 = expert(
        place, [b0, b_right, b_left], up, down, loads, [(i, 256) for i in range(3)], stores, [256] * 3, "experts_b013"
    )
    al[3], ar[3], y_b0, y_b1, y_b3 = fence(al[3], ar[3], y_b0, y_b1, y_b3)
    a_far0 = permute_z(al[3][:64], 1)
    a_far1 = permute_z(ar[3][64:128], -1)
    loads, stores = plan_b([((0, 0), (1, 0))])
    (y_b2,) = expert(place, [b_far0, b_far1], up, down, loads, [(0, 128)], stores, [256], "experts_b2")

    a_far0, a_far1, y_b2 = fence(a_far0, a_far1, y_b2)
    pieces = [*ar, a_far0, a_far1, al[3], al[2], al[1]]
    loads = [(d, 0, 128, d * 128, d) for d in range(4)]
    loads += [(4, 0, 64, 0, 4), (5, 0, 64, 64, 4)]
    loads += [(d + 1, 0, 128, (d - 4) * 128, d) for d in range(5, 8)]
    stores = [(0, 0, 128, q * 128, q) for q in range(4)]
    (y_a,) = expert(place, pieces, up, down, loads, [(d, 128) for d in range(4)], stores, [1024], "experts_a")
    y_a = [y_a[d * 128 : (d + 1) * 128] for d in range(8)]

    bl = permute_x(halves(y_b2)[0], 1)
    br = permute_x(halves(y_b2)[1], -1)
    al = permute_z(halves(y_a[4])[0], 1)
    ar = permute_z(halves(y_a[4])[1], -1)
    al, ar, bl, br = fence(al, ar, bl, br)
    al = permute_z(add_half(al, y_a[3], 0), 1)
    ar = permute_z(add_half(ar, y_a[5], 1), -1)
    bl = permute_x(add_half(bl, y_b1, 0), 1)
    br = permute_x(add_half(br, y_b3, 1), -1)
    al, ar = fence(al, ar)
    al = permute_z(add(al, y_a[2]), 1)
    ar = permute_z(add(ar, y_a[6]), -1)
    al, ar, bl, br = fence(al, ar, bl, br)
    s_b = (y_b0.astype(F32) + bl.astype(F32) + br.astype(F32)).astype(BF)
    s_b = [s_b[d * 32 : (d + 1) * 32] for d in range(8)]
    al = permute_z(add(al, y_a[1]), 1)
    ar = permute_z(add(ar, y_a[7]), -1)
    far = permute_z(s_b[4], 2)
    near = permute_z(s_b[3], 1)
    br = permute_z(s_b[5], -1)
    far, near, br = fence(far, near, br)
    bl = permute_z((far.astype(F32) + near.astype(F32) + s_b[2].astype(F32)).astype(BF), 1)
    br = permute_z(add(br, s_b[6]), -1)
    al, ar, bl, br = fence(al, ar, bl, br)
    s_a = y_a[0].astype(F32) + al.astype(F32) + ar.astype(F32)
    bl = permute_z(add(bl, s_b[1]), 1)
    br = permute_z(add(br, s_b[7]), -1)
    out_b = s_b[0].astype(F32) + bl.astype(F32) + br.astype(F32)
    far = [s_a[d * 32 : (d + 1) * 32].astype(BF) for d in range(1, 4)]
    got = [permute_x(far[0], 1), permute_x(far[1], 2), permute_x(far[2], 3)]
    out_a = s_a[:32] + got[0].astype(F32) + got[1].astype(F32) + got[2].astype(F32)
    return jnp.concatenate([out_a, out_b]).astype(BF)


def solution(mesh):
    fine = Mesh(mesh.devices.reshape(4, 4, 2, 4, 2), ("x", "zl", "zh", "y", "core"))
    rows = ("x", "zl", "y", "core")
    in_specs = (
        P(rows, "zh"),
        P(rows, None),
        P(rows, None),
        P(("x", "zl"), None, None, "zh"),
        P(("x", "zl"), "zh", None),
    )
    return jax.shard_map(
        local, mesh=fine, in_specs=in_specs, out_specs=P(rows, "zh"), check_vma=False
    )
```

```python
import functools

import jax
import jax.numpy as jnp
from jax import lax
from jax.experimental import pallas as pl
from jax.experimental.pallas import tpu as pltpu
from jax.sharding import Mesh
from jax.sharding import PartitionSpec as P

ZAX = ("zl", "zh")
BF = jnp.bfloat16
F32 = jnp.float32


def permute_x(v, step):
    return lax.ppermute(v, "x", [(i, (i + step) % 4) for i in range(4)])


def permute_z(v, step):
    index = lambda z: (z % 4) * 2 + z // 4
    return lax.ppermute(v, ZAX, [(index(z), index((z + step) % 8)) for z in range(8)])


def halves(v):
    n = v.shape[0] // 2
    return v[:n], v[n:]


def add(a, b):
    return (a.astype(F32) + b.astype(F32)).astype(BF)


def add_half(part, whole, which):
    w0, w1 = halves(whole)
    if which == 0:
        return jnp.concatenate([add(part, w0), w1])
    return jnp.concatenate([w0, add(part, w1)])


def fence(*values):
    return lax.optimization_barrier(values)


def weight_rows(dense):
    high = lax.reduce_precision(dense, 8, 7)
    rest = dense - high
    mid = lax.reduce_precision(rest, 8, 7)
    parts = jnp.stack([high, mid, rest - mid]).transpose(0, 2, 1).reshape(1, 1536)
    return jnp.broadcast_to(jnp.pad(parts.astype(BF), ((0, 0), (0, 512))), (8, 2048))


def pick_rows(blocks):
    row = lax.broadcasted_iota(jnp.int32, (8, 2048), 0)
    out = blocks[0]
    for r, block in enumerate(blocks[1:], 1):
        out = jnp.where(row == r, block, out)
    return out


def expert_kernel(loads, blocks, stores, n_in, n_out, place_ref, *refs):
    ins = refs[:n_in]
    up_ref, down_ref = refs[n_in : n_in + 2]
    outs = refs[n_in + 2 : n_in + 2 + n_out]
    x_buf, up_buf, down_buf, hidden, y_buf, rows_buf, w_buf, sem_x, sem_up, sem_down, sem_y = refs[n_in + 2 + n_out :]
    z, expert_num = place_ref[0], place_ref[1]

    def half_of(d):
        return lax.div(lax.rem(z + d, 8), 4)

    in_copies = [
        pltpu.make_async_copy(
            ins[ref].at[pl.ds(start, rows)],
            x_buf.at[pl.ds(row, rows), pl.ds(pl.multiple_of(half_of(d) * 2048, 2048), 2048)],
            sem_x,
        )
        for ref, start, rows, row, d in loads
    ] + [
        pltpu.make_async_copy(ins[ref].at[pl.ds(start, 8)], rows_buf.at[i], sem_x)
        for i, (ref, start) in enumerate(blocks)
    ]
    ups = [
        [
            pltpu.make_async_copy(
                up_ref.at[g, :, pl.ds(n * 256, 256)],
                up_buf.at[n, :, pl.ds(g * 256, 256)],
                sem_up.at[n, g],
            )
            for g in range(2)
        ]
        for n in range(2)
    ]
    downs = [
        pltpu.make_async_copy(
            down_ref.at[:, pl.ds(h * 2048, 2048)], down_buf.at[:, pl.ds(h * 2048, 2048)], sem_down.at[h]
        )
        for h in range(2)
    ]
    for c in [*in_copies, *ups[0], *ups[1], *downs]:
        c.start()
    for c in in_copies:
        c.wait()

    group = pl.multiple_of(lax.div(expert_num, 4) * 128, 128)
    lane = lax.broadcasted_iota(jnp.int32, (32, 128), 1)
    token = lax.broadcasted_iota(jnp.int32, (32, 128), 0)
    mine = lane == lax.rem(expert_num, 4) * 32 + token
    for i in range(len(blocks)):
        parts = [rows_buf[i, :, pl.ds(group + part * 512, 128)].astype(F32) for part in range(3)]
        total = parts[0] + parts[1] + parts[2]
        for j in range(4):
            picked = jnp.where(mine, jnp.broadcast_to(total[j : j + 1], (32, 128)), 0.0)
            w_buf[i * 128 + j * 32 : i * 128 + (j + 1) * 32, :] = jnp.broadcast_to(
                jnp.sum(picked, axis=1, keepdims=True), (32, 128)
            )

    for n in range(2):
        for c in ups[n]:
            c.wait()
        both = jnp.dot(x_buf[...], up_buf[n], preferred_element_type=F32)
        gate, up = both[:, :256], both[:, 256:]
        hidden[:, n * 256 : (n + 1) * 256] = (gate / (1.0 + jnp.exp(-gate)) * up).astype(BF)
    w = w_buf[:, :1]
    out_copies = []
    for h in range(2):
        downs[h].wait()
        for n in range(2):
            at = pl.ds(h * 2048 + n * 1024, 1024)
            y = jnp.dot(hidden[...], down_buf[:, at], preferred_element_type=F32)
            y_buf[:, at] = (y * w).astype(BF)
        for ref, start, rows, row, p in stores:
            d = p + 4 * lax.rem(half_of(p) + h, 2)
            c = pltpu.make_async_copy(
                y_buf.at[pl.ds(row, rows), pl.ds(h * 2048, 2048)],
                outs[ref].at[pl.ds(pl.multiple_of(start + d * rows, rows), rows)],
                sem_y,
            )
            c.start()
            out_copies.append(c)
    for c in out_copies:
        c.wait()


def expert(place, pieces, up, down, loads, blocks, stores, out_rows, name):
    n_in, n_out, rows = len(pieces), len(out_rows), len(blocks) * 128
    any_spec = pl.BlockSpec(memory_space=pl.ANY)
    return pl.pallas_call(
        functools.partial(expert_kernel, loads, blocks, stores, n_in, n_out),
        out_shape=[jax.ShapeDtypeStruct((r, 2048), BF) for r in out_rows],
        in_specs=[pl.BlockSpec(memory_space=pltpu.SMEM)] + [any_spec] * (n_in + 2),
        out_specs=[any_spec] * n_out,
        scratch_shapes=[
            pltpu.VMEM((rows, 4096), BF),
            pltpu.VMEM((2, 4096, 512), BF),
            pltpu.VMEM((512, 4096), BF),
            pltpu.VMEM((rows, 512), BF),
            pltpu.VMEM((rows, 4096), BF),
            pltpu.VMEM((len(blocks), 8, 2048), BF),
            pltpu.VMEM((rows, 128), F32),
            pltpu.SemaphoreType.DMA,
            pltpu.SemaphoreType.DMA((2, 2)),
            pltpu.SemaphoreType.DMA((2,)),
            pltpu.SemaphoreType.DMA,
        ],
        compiler_params=pltpu.CompilerParams(vmem_limit_bytes=48 << 20),
        name=name,
    )(place, *pieces, up, down)


def local(tokens, expert_ids, gate_weights, up_weights, down_weights):
    x, zl, zh = lax.axis_index("x"), lax.axis_index("zl"), lax.axis_index("zh")
    place = jnp.stack([zh * 4 + zl, x * 4 + zl]).astype(jnp.int32)
    picked = expert_ids[:, :, None] == jnp.arange(16, dtype=jnp.int32)
    dense = jnp.sum(jnp.where(picked, gate_weights[:, :, None], 0.0), axis=1)
    down = down_weights[0]

    b40 = jnp.concatenate([tokens[32:], weight_rows(dense[32:])])
    a40 = jnp.concatenate([tokens[:32], weight_rows(dense[:32])])
    b_by_z = [b40, permute_z(b40, -1), None, permute_z(b40, -3), None, permute_z(tokens[32:], 3), None, permute_z(tokens[32:], 1)]
    a1, a2, a3 = permute_x(a40, -1), permute_x(a40, 2), permute_x(a40, 1)
    b_by_z[2] = permute_z(b_by_z[1], -1)
    b_by_z[6], b_by_z[4] = halves(permute_z(jnp.concatenate([b_by_z[7], b_by_z[5]]), 1))

    a_by_x = [a40, a1, a2, a3]
    a_tokens = jnp.concatenate([v[:32] for v in a_by_x])
    a0 = jnp.concatenate([a_tokens, pick_rows([v[32:] for v in a_by_x])])
    al, ar = [a_tokens], [a0]
    up = jnp.transpose(up_weights[0], (1, 0, 2))
    al.append(permute_z(al[0], 1))
    ar.append(permute_z(ar[0], -1))
    b_rows = pick_rows([v[32:] for v in b_by_z[:4]])
    b0 = jnp.concatenate([v[:32] for v in b_by_z] + [b_rows])
    b_left = permute_x(b0, 1)
    b_right = permute_x(b0, -1)
    al[1], ar[1], up = fence(al[1], ar[1], up)
    al.append(permute_z(al[1], 1))
    ar.append(permute_z(ar[1], -1))

    def plan_b(sources):
        loads, stores = [], []
        for i, (near, far) in enumerate(sources):
            for q in range(4):
                loads.append((near[0], near[1] + q * 32, 32, i * 128 + q * 32, q))
                loads.append((far[0], far[1] + q * 32, 32, i * 128 + q * 32, q + 4))
                stores.append((i, 0, 32, i * 128 + q * 32, q))
        return loads, stores

    loads, stores = plan_b([((0, 0), (0, 128))])
    (y_b0,) = expert(place, [b0], up, down, loads, [(0, 256)], stores, [256], "experts_b0")
    al[2], ar[2], y_b0 = fence(al[2], ar[2], y_b0)
    al.append(permute_z(al[2], 1))
    ar.append(permute_z(ar[2], -1))
    b_far0 = permute_x(jnp.concatenate([b_left[:128], b_left[256:]]), 1)
    b_far1 = permute_x(b_right[128:256], -1)
    loads, stores = plan_b([((i, 0), (i, 128)) for i in range(2)])
    y_b1, y_b3 = expert(
        place, [b_right, b_left], up, down, loads, [(i, 256) for i in range(2)], stores, [256] * 2, "experts_b13"
    )
    al[3], ar[3], y_b1, y_b3 = fence(al[3], ar[3], y_b1, y_b3)
    a_far0 = permute_z(al[3][:64], 1)
    a_far1 = permute_z(ar[3][64:128], -1)
    loads, stores = plan_b([((0, 0), (1, 0))])
    (y_b2,) = expert(place, [b_far0, b_far1], up, down, loads, [(0, 128)], stores, [256], "experts_b2")

    a_far0, a_far1, y_b2 = fence(a_far0, a_far1, y_b2)
    pieces = [*ar, a_far0, a_far1, al[3], al[2], al[1]]
    loads = [(d, 0, 128, d * 128, d) for d in range(4)]
    loads += [(4, 0, 64, 0, 4), (5, 0, 64, 64, 4)]
    loads += [(d + 1, 0, 128, (d - 4) * 128, d) for d in range(5, 8)]
    stores = [(0, 0, 128, q * 128, q) for q in range(4)]
    (y_a,) = expert(place, pieces, up, down, loads, [(d, 128) for d in range(4)], stores, [1024], "experts_a")
    y_a = [y_a[d * 128 : (d + 1) * 128] for d in range(8)]

    bl = permute_x(halves(y_b2)[0], 1)
    br = permute_x(halves(y_b2)[1], -1)
    al = permute_z(halves(y_a[4])[0], 1)
    ar = permute_z(halves(y_a[4])[1], -1)
    al, ar, bl, br = fence(al, ar, bl, br)
    al = permute_z(add_half(al, y_a[3], 0), 1)
    ar = permute_z(add_half(ar, y_a[5], 1), -1)
    bl = permute_x(add_half(bl, y_b1, 0), 1)
    br = permute_x(add_half(br, y_b3, 1), -1)
    al, ar = fence(al, ar)
    al = permute_z(add(al, y_a[2]), 1)
    ar = permute_z(add(ar, y_a[6]), -1)
    al, ar, bl, br = fence(al, ar, bl, br)
    s_b = (y_b0.astype(F32) + bl.astype(F32) + br.astype(F32)).astype(BF)
    s_b = [s_b[d * 32 : (d + 1) * 32] for d in range(8)]
    al = permute_z(add(al, y_a[1]), 1)
    ar = permute_z(add(ar, y_a[7]), -1)
    far = permute_z(s_b[4], 2)
    near = permute_z(s_b[3], 1)
    br = permute_z(s_b[5], -1)
    far, near, br = fence(far, near, br)
    bl = permute_z((far.astype(F32) + near.astype(F32) + s_b[2].astype(F32)).astype(BF), 1)
    br = permute_z(add(br, s_b[6]), -1)
    al, ar, bl, br = fence(al, ar, bl, br)
    s_a = y_a[0].astype(F32) + al.astype(F32) + ar.astype(F32)
    bl = permute_z(add(bl, s_b[1]), 1)
    br = permute_z(add(br, s_b[7]), -1)
    out_b = s_b[0].astype(F32) + bl.astype(F32) + br.astype(F32)
    far = [s_a[d * 32 : (d + 1) * 32].astype(BF) for d in range(1, 4)]
    got = [permute_x(far[0], 1), permute_x(far[1], 2), permute_x(far[2], 3)]
    out_a = s_a[:32] + got[0].astype(F32) + got[1].astype(F32) + got[2].astype(F32)
    return jnp.concatenate([out_a, out_b]).astype(BF)


def solution(mesh):
    fine = Mesh(mesh.devices.reshape(4, 4, 2, 4, 2), ("x", "zl", "zh", "y", "core"))
    rows = ("x", "zl", "y", "core")
    in_specs = (
        P(rows, "zh"),
        P(rows, None),
        P(rows, None),
        P(("x", "zl"), None, None, "zh"),
        P(("x", "zl"), "zh", None),
    )
    return jax.shard_map(
        local, mesh=fine, in_specs=in_specs, out_specs=P(rows, "zh"), check_vma=False
    )
```
